256 devices in a mesh: rep: 16 (over z, core), exp: 16 (over y, x).
Axes of the slice: x: 4, y: 4, z: 8, core: 2. Of those that a mesh axis runs over, the one named last changes fastest.
Arguments:
- latents: float32 [32, 32, 2048], P('rep', None, 'exp'), may hold values from -6 to 6
- latent_mean: float32 [32, 32, 2048], P('rep', None, 'exp'), may hold values from -0.12 to 0.12
- latent_square: float32 [32, 32, 2048], P('rep', None, 'exp'), may hold values from 0.0001 to 0.01
- weight_one: bfloat16 [64, 64, 256], P('exp'), may hold values from -0.75 to 0.75
- weight_two: bfloat16 [64, 256, 256], P('exp'), may hold values from -0.375 to 0.375
- weight_three: bfloat16 [64, 3, 256], P('exp'), may hold values from -0.375 to 0.375
- dir_table: bfloat16 [256, 32], replicated, may hold values from -6 to 6
- materials: int32 [524288, 1], P(('rep', 'exp')), may hold values from 0 to 63; in each aligned block of 2048 rows (0 to 2047, 2048 to 4095, ...) at most 64 rows name the same one
- tile_ids: int32 [524288], P(('rep', 'exp')), may hold values from 0 to 1
- texel_ids: int32 [524288], P(('rep', 'exp')), may hold values from 0 to 2047
- dir_ids: int32 [524288], P(('rep', 'exp')), may hold values from 0 to 255
- targets: float32 [3, 524288], P(None, ('rep', 'exp')), may hold values from -12 to 12
Outputs:
- new_latents: float32 [32, 32, 2048], P('rep', None, 'exp')
- new_mean: float32 [32, 32, 2048], P('rep', None, 'exp')
- new_square: float32 [32, 32, 2048], P('rep', None, 'exp')
- predictions: float32 [3, 524288], P(None, ('rep', 'exp'))
- grad_one: float32 [64, 64, 256], P('exp')
- grad_two: float32 [64, 256, 256], P('exp')
- grad_three: float32 [64, 3, 256], P('exp')
The draws below stay inside these ranges and needn't reach their ends.
Inputs may be any that keep to these rules, and one draw needn't show every extreme that they name: `materials`: within the rows of one device no material is named by more than 64 rows, a bound that some block reaches.
All inputs are finite; a program needn't handle non-finite values.
Results may differ from the reference program's by a relative error of at most 0.02.
Values may be sent and summed in bfloat16 or wider, within the bound.
No kernel may reach another device: no remote copies, remote signals or barrier semaphores. Data moves between devices by JAX's collectives and lax.ppermute only.
A program may use at most 64 MiB of HBM per device.

```python
import math
import jax
import jax.numpy as jnp
import numpy as np
from jax import lax

LAT = 32
DIRF = 32
HID = 256
OUTC = 3
NDIR = 256
TILE_DEV = 2
TEXELS = 2048
S_DEV = 2048
EXPERTS = 64
CAP = 64
SAMPLES = 524288
TILES = 32
N_REP = 16
N_EXP = 16


def set_ends(values, key, low, top_value):
    extent = values.shape
    index_at = [jax.random.randint(jax.random.fold_in(key, axis), (), 0, extent[axis]) for axis in range(len(extent))]
    values = values.at[tuple(index_at)].set(low)
    longest = extent.index(max(extent))
    index_at[longest] = (index_at[longest] + 1) % extent[longest]
    return values.at[tuple(index_at)].set(top_value)


def block_levels(own_key, shape, cuts, smallest, top_value):
    gain, own = 1.0, jax.random.fold_in(own_key, 6)
    for dim, blocks in cuts:
        steps = jnp.exp(jax.random.uniform(jax.random.fold_in(own, dim), (blocks,), jnp.float32, smallest / len(cuts), top_value / len(cuts)))
        gain = gain * jnp.repeat(steps, shape[dim] // blocks).reshape([-1 if axis == dim else 1 for axis in range(len(shape))])
    return gain


def routed_block(key, own, number, rows, count, top, bound, slope):
    sequence = jax.random.permutation(key, count)
    packed, common = shares(count, rows * top, bound, slope, True), shares(count, rows * top, bound, slope, False)
    places = jnp.arange(count)

    def named(tallies, rotation):
        used = int((tallies > 0).sum())
        fixed = max(1, used // 4)
        moved = fixed + (places - fixed + rotation * (used - fixed)) % max(1, count - fixed)
        return jnp.zeros((count,), jnp.int32).at[sequence[jnp.where(places < fixed, places, moved)]].set(jnp.asarray(tallies, jnp.int32))

    tallies = jnp.where(number % 4 == 0, named(packed, number // 4), named(common, number - number // 4 - 1))
    mixed = jax.random.permutation(jax.random.fold_in(own, 3), count)
    source_of, receiver = mixed[0:count // 2 * 2:2], mixed[1:count // 2 * 2:2]
    room = jnp.minimum(tallies[source_of] - 1, bound - tallies[receiver]) // 2
    room = jnp.where((source_of == sequence[0]) | (receiver == sequence[0]) | (tallies[receiver] == 0), 0, jnp.maximum(room, 0))
    moved = jax.random.randint(jax.random.fold_in(own, 4), (count // 2,), 0, 1 << 20) % (room + 1)
    tallies = tallies.at[source_of].add(-moved).at[receiver].add(moved)
    items = jnp.searchsorted(jnp.cumsum(tallies), jnp.arange(rows * top), side="right").astype(jnp.int32)
    listing = items.reshape(top, rows).T
    listing = listing[jax.random.permutation(jax.random.fold_in(own, 1), rows)]
    rotation = jax.random.randint(jax.random.fold_in(own, 2), (rows, 1), 0, top)
    return jnp.take_along_axis(listing, (jnp.arange(top)[None, :] + rotation) % top, axis=1)


def shares(number_of, total, bound, lean, full):
    weights = [(1 << 20) // math.isqrt(rank ** lean) + 1 for rank in range(1, number_of + 1)]
    largest = bound if full else min(bound, max(-(-total // number_of), total * weights[0] // sum(weights)))
    least = 1 if total - largest >= number_of - 1 else 0
    counts, rest = [largest] + [least] * (number_of - 1), total - largest - least * (number_of - 1)
    while rest > 0:
        candidates = [i for i in range(1, number_of) if counts[i] < largest] or [i for i in range(1, number_of) if counts[i] < bound]
        whole, budget = sum([weights[i] for i in candidates]), rest
        for i in candidates:
            more = min(bound - counts[i], max(1, budget * weights[i] // whole), rest)
            counts[i] = counts[i] + more
            rest = rest - more
    return np.array(counts)


def normal_values(key, extent, deviation, bound, pieces=(), kind=jnp.bfloat16):
    array = jax.random.normal(key, extent, jnp.float32) * deviation
    if len(pieces) > 0:
        array = block_levels(key, extent, pieces, -0.22, 0.18) * array
    return jnp.clip(array, min=-bound, max=bound).astype(kind)


def setup_inputs(seed: int = 0) -> dict:
    keys = jax.random.split(jax.random.key(seed), 13)
    latents = normal_values(keys[0], (TILES, LAT, TEXELS), 1.0, 6.0, ((0, 16), (2, 16)), jnp.float32)
    latent_mean = normal_values(keys[1], (TILES, LAT, TEXELS), 0.02, 0.12, ((0, 16), (2, 16)), jnp.float32)
    latent_square = jnp.clip(jnp.exp(math.log(0.01) - 4.6051702 * jax.random.uniform(keys[2], (TILES, LAT, TEXELS), jnp.float32) ** block_levels(keys[2], (TILES, LAT, TEXELS), ((0, 16), (2, 16)), -0.2, 0.2)), 0.0001, 0.01)
    weight_one = normal_values(keys[3], (EXPERTS, LAT + DIRF, HID), (LAT + DIRF) ** -0.5, 0.75, ((0, 16),))
    weight_two = normal_values(keys[4], (EXPERTS, HID, HID), HID ** -0.5, 0.375, ((0, 16),))
    weight_three = normal_values(keys[5], (EXPERTS, OUTC, HID), HID ** -0.5, 0.375, ((0, 16),))
    dir_table = normal_values(keys[6], (NDIR, DIRF), 1.0, 6.0)
    materials_keys = jax.random.split(jax.random.fold_in(keys[7], 1), SAMPLES // S_DEV)
    materials_turns = jax.random.permutation(jax.random.fold_in(keys[7], 3), SAMPLES // S_DEV)
    materials = jax.vmap(lambda own, number: routed_block(jax.random.fold_in(keys[7], 2), own, number, S_DEV, EXPERTS, 1, CAP, 2))(materials_keys, materials_turns).reshape((SAMPLES, 1))
    tile_ids = set_ends(jax.random.randint(keys[8], (SAMPLES,), 0, TILE_DEV), jax.random.fold_in(keys[8], 1), 0, TILE_DEV - 1).astype(jnp.int32)
    texel_ids = set_ends(jax.random.randint(keys[9], (SAMPLES,), 0, TEXELS), jax.random.fold_in(keys[9], 1), 0, TEXELS - 1).astype(jnp.int32)
    dir_ids = set_ends(jax.random.randint(keys[10], (SAMPLES,), 0, NDIR), jax.random.fold_in(keys[10], 1), 0, NDIR - 1).astype(jnp.int32)
    targets = normal_values(keys[11], (OUTC, SAMPLES), 2.0, 12.0, ((1, 256),), jnp.float32)
    return dict(latents=latents, latent_mean=latent_mean, latent_square=latent_square, weight_one=weight_one, weight_two=weight_two, weight_three=weight_three, dir_table=dir_table, materials=materials, tile_ids=tile_ids, texel_ids=texel_ids, dir_ids=dir_ids, targets=targets)


decay_one = 0.9
decay_two = 0.99
step_rate = 0.05
epsilon = 1e-08

def silu_slope(preact):
    sigmoid_v = jax.nn.sigmoid(preact)
    return sigmoid_v * (1.0 + preact * (1.0 - sigmoid_v))

def expert_step(inputs, target_rows, layer_one, layer_two, layer_three):
    pre_one = jnp.dot(inputs, layer_one, preferred_element_type=jnp.float32)
    act_one = jax.nn.silu(pre_one).astype(jnp.bfloat16)
    pre_two = jnp.dot(act_one, layer_two, preferred_element_type=jnp.float32)
    act_two = jax.nn.silu(pre_two).astype(jnp.bfloat16)
    predicted = lax.dot_general(act_two, layer_three, (((1,), (1,)), ((), ())), preferred_element_type=jnp.float32)
    misfit = (predicted - target_rows).astype(jnp.bfloat16)
    grad_three = lax.dot_general(misfit, act_two, (((0,), (0,)), ((), ())), preferred_element_type=jnp.float32)
    back_two = jnp.dot(misfit, layer_three, preferred_element_type=jnp.float32)
    delta_two = (back_two * silu_slope(pre_two)).astype(jnp.bfloat16)
    grad_two = lax.dot_general(act_one, delta_two, (((0,), (0,)), ((), ())), preferred_element_type=jnp.float32)
    back_one = lax.dot_general(delta_two, layer_two, (((1,), (1,)), ((), ())), preferred_element_type=jnp.float32)
    delta_one = (back_one * silu_slope(pre_one)).astype(jnp.bfloat16)
    grad_one = lax.dot_general(inputs, delta_one, (((0,), (0,)), ((), ())), preferred_element_type=jnp.float32)
    latent_part = layer_one[:LAT]
    latent_rows = lax.dot_general(delta_one, latent_part, (((1,), (1,)), ((), ())), preferred_element_type=jnp.float32)
    return (latent_rows.astype(jnp.bfloat16), predicted, grad_one, grad_two, grad_three)

def reference(latents, latent_mean, latent_square, weight_one, weight_two, weight_three, dir_table, materials, tile_ids, texel_ids, dir_ids, targets):
    devices = N_REP * N_EXP
    samples = materials.shape[0]
    material = materials[:, 0]
    one_hot = (material[:, None] == jnp.arange(EXPERTS, dtype=jnp.int32)[None, :]).astype(jnp.int32)
    counted = jnp.cumsum(one_hot.reshape(devices, S_DEV, EXPERTS), axis=1).reshape(samples, EXPERTS)
    position = lax.optimization_barrier(jnp.sum((counted - 1) * one_hot, axis=1)).astype(jnp.int32)
    device_block = (jnp.arange(samples, dtype=jnp.int32) // S_DEV).astype(jnp.int32)
    slot_index = (device_block * CAP + position).astype(jnp.int32)
    rep_group = (device_block // N_EXP).astype(jnp.int32)
    tile_global = (rep_group * TILE_DEV + tile_ids).astype(jnp.int32)
    latent_bf = latents.astype(jnp.bfloat16)
    sample_latent = latent_bf[tile_global, :, texel_ids]
    feature_rows = jnp.concatenate([sample_latent, dir_table[dir_ids]], axis=1)
    target_cols = targets.T
    total_slots = devices * CAP

    def per_expert(expert):
        target_slot = jnp.where(material == expert, slot_index, total_slots).astype(jnp.int32)
        inputs = jnp.zeros((total_slots, feature_rows.shape[1]), jnp.bfloat16).at[target_slot].set(feature_rows, mode='drop')
        wanted = jnp.zeros((total_slots, OUTC), jnp.float32).at[target_slot].set(target_cols, mode='drop')
        return expert_step(inputs, wanted, weight_one[expert], weight_two[expert], weight_three[expert])
    latent_rows, predicted, grad_one, grad_two, grad_three = lax.map(per_expert, jnp.arange(EXPERTS, dtype=jnp.int32))
    sample_grad = latent_rows[material, slot_index].astype(jnp.float32)
    sample_pred = predicted[material, slot_index]
    texel_grad = jnp.zeros(latents.shape, jnp.float32).at[tile_global, :, texel_ids].add(sample_grad)
    new_mean = decay_one * latent_mean + (1.0 - decay_one) * texel_grad
    new_square = decay_two * latent_square + (1.0 - decay_two) * texel_grad * texel_grad
    new_latents = latents - step_rate * new_mean / (jnp.sqrt(new_square) + epsilon)
    return (new_latents, new_mean, new_square, sample_pred.T, grad_one, grad_two, grad_three)
```

```python
import jax
import jax.numpy as jnp
from jax import lax
from jax.experimental import pallas as pl
from jax.experimental.pallas import tpu as pltpu
from jax.sharding import PartitionSpec as P

LAT = 32
HID = 256
OUTC = 3
LANES = 128
N_EXP = 16
N_REP = 16
CAP = 64
ROWS = 2048
CHUNKS = ROWS // LANES
SLOTS = N_EXP * CAP
GROUPS = 16
TEX_ROWS = 64
SEND_ROWS = TEX_ROWS + 16
GRAD_ROWS = 168

decay_one = 0.9
decay_two = 0.99
step_rate = 0.05
epsilon = 1e-08

f32 = jnp.float32
bf16 = jnp.bfloat16


def dot(a, b):
    return jnp.dot(a, b, preferred_element_type=f32)


def dot_nt(a, b):
    return lax.dot_general(a, b, (((1,), (1,)), ((), ())), preferred_element_type=f32)


def iota(shape, dim):
    return lax.broadcasted_iota(jnp.int32, shape, dim)


def hot(index, count, start=0):
    same = iota((count, index.shape[1]), 0) + start == index
    return jnp.where(same, 1.0, 0.0).astype(bf16)


def route_kernel(mat, tile, texel, direction, targets, latents, send, slot):
    material = mat[...]
    hots = [hot(material[i : i + 1], 64) for i in range(CHUNKS)]
    upper = jnp.where(iota((LANES, LANES), 0) <= iota((LANES, LANES), 1), 1.0, 0.0).astype(bf16)
    counted = dot(jnp.concatenate(hots, axis=0), upper)
    before = jnp.zeros((64, 1), f32)
    places = []
    for i in range(CHUNKS):
        here = counted[i * 64 : (i + 1) * 64]
        places.append(jnp.sum(hots[i].astype(f32) * (here + before), axis=0, keepdims=True))
        before = before + here[:, LANES - 1 :]
    place = jnp.concatenate(places, axis=0).astype(jnp.int32) - 1
    lane = (material & 1) * CAP + place
    pair = material >> 1
    slot[...] = pair * LANES + lane
    texels = texel[...]
    block = texels >> 8
    high = (block * 2 + tile[...] + 1).astype(f32)
    low = (texels & 255).astype(f32)
    heading = (direction[...] + 1).astype(f32)
    values = []
    lanes_hot = []
    for i in range(CHUNKS):
        row = slice(i, i + 1)
        val = jnp.concatenate(
            [
                targets[:, i * LANES : (i + 1) * LANES],
                high[row],
                low[row],
                heading[row],
                jnp.zeros((2, LANES), f32),
            ],
            axis=0,
        )
        parts = [jnp.where(pair[row] == g, val, 0.0) for g in range(32)]
        values.append(jnp.concatenate(parts, axis=0).astype(bf16))
        lanes_hot.append(hot(lane[row], LANES))
    out = dot_nt(jnp.concatenate(values, axis=1), jnp.concatenate(lanes_hot, axis=1)).astype(bf16)
    own = latents[...].astype(bf16)
    for j in range(N_EXP):
        send[j, :TEX_ROWS] = own
        send[j, TEX_ROWS:] = out[j * 16 : (j + 1) * 16]


def experts_kernel(recv, w_one, w_one_t, w_two, w_two_t, w_three, w_three_t, dir_t, back, grads, tex, acc):
    for b in range(8):
        for h in range(2):
            tex[b * TEX_ROWS : (b + 1) * TEX_ROWS, h * LANES : (h + 1) * LANES] = recv[2 * b + h, :TEX_ROWS]
    acc[...] = jnp.zeros(acc.shape, f32)
    left = iota((8, LANES), 1) < CAP
    for h in range(2):
        sides = ([], [])
        for j in range(N_EXP // 2):
            first = recv[2 * j, TEX_ROWS + 8 * h : TEX_ROWS + 8 * h + 8].astype(f32)
            second = recv[2 * j + 1, TEX_ROWS + 8 * h : TEX_ROWS + 8 * h + 8].astype(f32)
            sides[0].append(jnp.where(left, first, pltpu.roll(second, CAP, 1)))
            sides[1].append(jnp.where(left, pltpu.roll(first, CAP, 1), second))
        preds = []
        for b in range(2):
            e = 2 * h + b
            rows = jnp.concatenate(sides[b], axis=1)
            group = rows[3:4].astype(jnp.int32)
            low_hot = hot(rows[4:5].astype(jnp.int32), 256)
            dir_hot = hot(rows[5:6].astype(jnp.int32), 256, 1)
            picked = dot(tex[...], low_hot)
            lat = jnp.zeros((LAT, SLOTS), f32)
            for r in range(GROUPS):
                lat = lat + jnp.where(group == r + 1, picked[r * LAT : (r + 1) * LAT], 0.0)
            x = jnp.concatenate([lat, dot(dir_t[...], dir_hot)], axis=0).astype(bf16)
            pre_one = dot(w_one_t[e], x)
            sig_one = 0.5 * jnp.tanh(0.5 * pre_one) + 0.5
            raw_one = pre_one * sig_one
            act_one = raw_one.astype(bf16)
            slope_one = sig_one + raw_one * (1.0 - sig_one)
            pre_two = dot(w_two_t[e], act_one)
            sig_two = 0.5 * jnp.tanh(0.5 * pre_two) + 0.5
            raw_two = pre_two * sig_two
            act_two = raw_two.astype(bf16)
            slope_two = sig_two + raw_two * (1.0 - sig_two)
            pred = dot(w_three[e], act_two)
            preds.append(pred)
            misfit = jnp.where(iota((8, SLOTS), 0) < OUTC, pred - rows, 0.0).astype(bf16)
            delta_two = (dot(w_three_t[e], misfit) * slope_two).astype(bf16)
            delta_one = (dot(w_two[e], delta_two) * slope_one).astype(bf16)
            grad_three = dot_nt(misfit, act_two).astype(bf16)
            grad_two = dot_nt(act_one, delta_two).astype(bf16)
            grad_one = dot_nt(x, delta_one).astype(bf16)
            for q in range(4):
                for s in range(2):
                    cols = slice(s * LANES, (s + 1) * LANES)
                    grads[4 * e + q, s * 64 : (s + 1) * 64] = grad_two[q * 64 : (q + 1) * 64, cols]
                    grads[4 * e + q, 128 + s * 16 : 128 + (s + 1) * 16] = grad_one[q * 16 : (q + 1) * 16, cols]
                grads[4 * e + q, 160:168] = grad_three[:, (q % 2) * LANES : (q % 2 + 1) * LANES]
            rows_back = dot(w_one[e, :LAT], delta_one)
            spread = [jnp.where(group == r + 1, rows_back, 0.0).astype(bf16) for r in range(GROUPS)]
            acc[...] += dot_nt(jnp.concatenate(spread, axis=0), low_hot)
        for j in range(N_EXP // 2):
            one = preds[0][:, j * LANES : (j + 1) * LANES]
            two = preds[1][:, j * LANES : (j + 1) * LANES]
            back[2 * j, TEX_ROWS + 8 * h : TEX_ROWS + 8 * h + 8] = jnp.where(
                left, one, pltpu.roll(two, CAP, 1)
            ).astype(bf16)
            back[2 * j + 1, TEX_ROWS + 8 * h : TEX_ROWS + 8 * h + 8] = jnp.where(
                left, pltpu.roll(one, CAP, 1), two
            ).astype(bf16)
    for b in range(8):
        for h in range(2):
            back[2 * b + h, :TEX_ROWS] = acc[
                b * TEX_ROWS : (b + 1) * TEX_ROWS, h * LANES : (h + 1) * LANES
            ].astype(bf16)


def finish_kernel(got, slot, latents, mean, square, new_latents, new_mean, new_square, predictions):
    texel_grad = jnp.zeros((TEX_ROWS, LANES), f32)
    for j in range(N_EXP):
        texel_grad = texel_grad + got[j, :TEX_ROWS].astype(f32)
    next_mean = decay_one * mean[...] + (1.0 - decay_one) * texel_grad
    next_square = decay_two * square[...] + (1.0 - decay_two) * texel_grad * texel_grad
    new_mean[...] = next_mean
    new_square[...] = next_square
    new_latents[...] = latents[...] - step_rate * next_mean / (jnp.sqrt(next_square) + epsilon)
    table = jnp.concatenate([got[j, TEX_ROWS:] for j in range(N_EXP)], axis=0)
    place = slot[...]
    lane = place & (LANES - 1)
    pair = place >> 7
    for i in range(CHUNKS):
        row = slice(i, i + 1)
        picked = dot(table, hot(lane[row], LANES))
        total = jnp.zeros((8, LANES), f32)
        for g in range(32):
            total = total + jnp.where(pair[row] == g, picked[g * 8 : (g + 1) * 8], 0.0)
        predictions[:, i * LANES : (i + 1) * LANES] = total[:OUTC]


def unpack_kernel(packed, grad_one, grad_two, grad_three):
    for e in range(4):
        for q in range(4):
            for s in range(2):
                cols = slice(s * LANES, (s + 1) * LANES)
                grad_two[e, q * 64 : (q + 1) * 64, cols] = packed[4 * e + q, s * 64 : (s + 1) * 64].astype(f32)
                grad_one[e, q * 16 : (q + 1) * 16, cols] = packed[
                    4 * e + q, 128 + s * 16 : 128 + (s + 1) * 16
                ].astype(f32)
        for s in range(2):
            grad_three[e, :, s * LANES : (s + 1) * LANES] = packed[4 * e + s, 160:168].astype(f32)[:OUTC]


def call(kernel, outs, scratch=()):
    return pl.pallas_call(
        kernel,
        out_shape=outs,
        scratch_shapes=list(scratch),
        compiler_params=pltpu.CompilerParams(vmem_limit_bytes=48 << 20),
    )


def shape(dims, kind=f32):
    return jax.ShapeDtypeStruct(dims, kind)


def on_device(
    latents,
    latent_mean,
    latent_square,
    weight_one,
    weight_two,
    weight_three,
    dir_table,
    materials,
    tile_ids,
    texel_ids,
    dir_ids,
    targets,
):
    flat = lambda a: a.reshape(TEX_ROWS, LANES)
    rows = lambda a: a.reshape(CHUNKS, LANES)
    send, slot = call(
        route_kernel,
        (shape((N_EXP, SEND_ROWS, LANES), bf16), shape((CHUNKS, LANES), jnp.int32)),
    )(rows(materials), rows(tile_ids), rows(texel_ids), rows(dir_ids), targets, flat(latents))
    recv = lax.all_to_all(send, "exp", 0, 0, tiled=True)
    three = jnp.pad(weight_three, ((0, 0), (0, 8 - OUTC), (0, 0)))
    back, grads = call(
        experts_kernel,
        (shape((N_EXP, SEND_ROWS, LANES), bf16), shape((N_REP, GRAD_ROWS, LANES), bf16)),
        [pltpu.VMEM((GROUPS * LAT, 256), bf16), pltpu.VMEM((GROUPS * LAT, 256), f32)],
    )(
        recv,
        weight_one,
        jnp.swapaxes(weight_one, 1, 2),
        weight_two,
        jnp.swapaxes(weight_two, 1, 2),
        three,
        jnp.swapaxes(three, 1, 2),
        dir_table.T,
    )
    parts = lax.all_to_all(grads, "rep", 0, 0, tiled=True)
    got = lax.all_to_all(back, "exp", 0, 0, tiled=True)
    own = jnp.sum(parts.astype(f32), axis=0).astype(bf16)
    packed = lax.all_gather(own, "rep", axis=0, tiled=False)
    new_latents, new_mean, new_square, predictions = call(
        finish_kernel,
        (shape((TEX_ROWS, LANES)), shape((TEX_ROWS, LANES)), shape((TEX_ROWS, LANES)), shape((OUTC, ROWS))),
    )(got, slot, flat(latents), flat(latent_mean), flat(latent_square))
    grad_one, grad_two, grad_three = call(
        unpack_kernel,
        (shape(weight_one.shape), shape(weight_two.shape), shape(weight_three.shape)),
    )(packed)
    whole = lambda a: a.reshape(latents.shape)
    return (
        whole(new_latents),
        whole(new_mean),
        whole(new_square),
        predictions,
        grad_one,
        grad_two,
        grad_three,
    )


def solution(mesh):
    in_specs = (
        P("rep", None, "exp"),
        P("rep", None, "exp"),
        P("rep", None, "exp"),
        P("exp", None, None),
        P("exp", None, None),
        P("exp", None, None),
        P(),
        P(("rep", "exp"), None),
        P(("rep", "exp")),
        P(("rep", "exp")),
        P(("rep", "exp")),
        P(None, ("rep", "exp")),
    )
    out_specs = (
        P("rep", None, "exp"),
        P("rep", None, "exp"),
        P("rep", None, "exp"),
        P(None, ("rep", "exp")),
        P("exp", None, None),
        P("exp", None, None),
        P("exp", None, None),
    )
    return jax.shard_map(on_device, mesh=mesh, in_specs=in_specs, out_specs=out_specs, check_vma=False)
```

```python
import jax
import jax.numpy as jnp
from jax import lax
from jax.experimental import pallas as pl
from jax.experimental.pallas import tpu as pltpu
from jax.sharding import PartitionSpec as P

LAT = 32
HID = 256
OUTC = 3
LANES = 128
N_EXP = 16
N_REP = 16
CAP = 64
ROWS = 2048
CHUNKS = ROWS // LANES
SLOTS = N_EXP * CAP
GROUPS = 16
TEX_ROWS = 64
SEND_ROWS = TEX_ROWS + 16
GRAD_ROWS = 168

decay_one = 0.9
decay_two = 0.99
step_rate = 0.05
epsilon = 1e-08

f32 = jnp.float32
bf16 = jnp.bfloat16


def dot(a, b):
    return jnp.dot(a, b, preferred_element_type=f32)


def dot_nt(a, b):
    return lax.dot_general(a, b, (((1,), (1,)), ((), ())), preferred_element_type=f32)


def iota(shape, dim):
    return lax.broadcasted_iota(jnp.int32, shape, dim)


def hot(index, count, start=0):
    same = iota((count, index.shape[1]), 0) + start == index
    return jnp.where(same, 1.0, 0.0).astype(bf16)


def route_kernel(mat, tile_in, texel_in, direction_in, targets_in, latents_in, send, slot, *scratch):
    material_in, tile, texel, direction, targets, latents, sems = scratch
    copies = [
        pltpu.make_async_copy(source, target, sems.at[n])
        for n, (source, target) in enumerate(
            [
                (mat, material_in),
                (tile_in, tile),
                (texel_in, texel),
                (direction_in, direction),
                (targets_in, targets),
                (latents_in, latents),
            ]
        )
    ]
    for copy in copies:
        copy.start()
    for copy in copies:
        copy.wait()
    material = material_in[...]
    hots = [hot(material[i : i + 1], 64) for i in range(CHUNKS)]
    upper = jnp.where(iota((LANES, LANES), 0) <= iota((LANES, LANES), 1), 1.0, 0.0).astype(bf16)
    counted = dot(jnp.concatenate(hots, axis=0), upper)
    before = jnp.zeros((64, 1), f32)
    places = []
    for i in range(CHUNKS):
        here = counted[i * 64 : (i + 1) * 64]
        places.append(jnp.sum(hots[i].astype(f32) * (here + before), axis=0, keepdims=True))
        before = before + here[:, LANES - 1 :]
    place = jnp.concatenate(places, axis=0).astype(jnp.int32) - 1
    lane = (material & 1) * CAP + place
    pair = material >> 1
    slot[...] = pair * LANES + lane
    texels = texel[...]
    block = texels >> 8
    high = (block * 2 + tile[...] + 1).astype(f32)
    low = (texels & 255).astype(f32)
    heading = (direction[...] + 1).astype(f32)
    values = []
    lanes_hot = []
    for i in range(CHUNKS):
        row = slice(i, i + 1)
        val = jnp.concatenate(
            [
                targets[:, i * LANES : (i + 1) * LANES],
                high[row],
                low[row],
                heading[row],
                jnp.zeros((2, LANES), f32),
            ],
            axis=0,
        )
        parts = [jnp.where(pair[row] == g, val, 0.0) for g in range(32)]
        values.append(jnp.concatenate(parts, axis=0).astype(bf16))
        lanes_hot.append(hot(lane[row], LANES))
    out = dot_nt(jnp.concatenate(values, axis=1), jnp.concatenate(lanes_hot, axis=1)).astype(bf16)
    own = latents[...].astype(bf16)
    for j in range(N_EXP):
        send[j, :TEX_ROWS] = own
        send[j, TEX_ROWS:] = out[j * 16 : (j + 1) * 16]


def half_kernel(
    half, recv, w_one, w_one_t, w_two, w_two_t, w_three, w_three_t, dir_t, grads, back, preds, index, tex
):
    h = half[0]
    for b in range(8):
        for s in range(2):
            tex[b * TEX_ROWS : (b + 1) * TEX_ROWS, s * LANES : (s + 1) * LANES] = recv[2 * b + s, :TEX_ROWS]
    left = iota((8, LANES), 1) < CAP
    sides = ([], [])
    for j in range(N_EXP // 2):
        both = [recv[2 * j + s, TEX_ROWS:].astype(f32) for s in range(2)]
        first, second = [jnp.where(h == 0, v[:8], v[8:]) for v in both]
        sides[0].append(jnp.where(left, first, pltpu.roll(second, CAP, 1)))
        sides[1].append(jnp.where(left, pltpu.roll(first, CAP, 1), second))
    for b in range(2):
        e = 2 * h + b
        rows = jnp.concatenate(sides[b], axis=1)
        index[b] = rows
        group = rows[3:4].astype(jnp.int32)
        low_hot = hot(rows[4:5].astype(jnp.int32), 256)
        dir_hot = hot(rows[5:6].astype(jnp.int32), 256, 1)
        picked = dot(tex[...], low_hot)
        lat = jnp.zeros((LAT, SLOTS), f32)
        for r in range(GROUPS):
            lat = lat + jnp.where(group == r + 1, picked[r * LAT : (r + 1) * LAT], 0.0)
        x = jnp.concatenate([lat, dot(dir_t[...], dir_hot)], axis=0).astype(bf16)
        pre_one = dot(w_one_t[e], x)
        sig_one = 0.5 * jnp.tanh(0.5 * pre_one) + 0.5
        raw_one = pre_one * sig_one
        act_one = raw_one.astype(bf16)
        slope_one = sig_one + raw_one * (1.0 - sig_one)
        pre_two = dot(w_two_t[e], act_one)
        sig_two = 0.5 * jnp.tanh(0.5 * pre_two) + 0.5
        raw_two = pre_two * sig_two
        act_two = raw_two.astype(bf16)
        slope_two = sig_two + raw_two * (1.0 - sig_two)
        pred = dot(w_three[e], act_two)
        preds[b] = pred
        misfit = jnp.where(iota((8, SLOTS), 0) < OUTC, pred - rows, 0.0).astype(bf16)
        delta_two = (dot(w_three_t[e], misfit) * slope_two).astype(bf16)
        delta_one = (dot(w_two[e], delta_two) * slope_one).astype(bf16)
        grad_three = dot_nt(misfit, act_two).astype(grads.dtype)
        grad_two = dot_nt(act_one, delta_two).astype(grads.dtype)
        grad_one = dot_nt(x, delta_one).astype(grads.dtype)
        for q in range(4):
            n = 4 * b + q
            for s in range(2):
                cols = slice(s * LANES, (s + 1) * LANES)
                grads[n, s * 64 : (s + 1) * 64] = grad_two[q * 64 : (q + 1) * 64, cols]
                grads[n, 128 + s * 16 : 128 + (s + 1) * 16] = grad_one[q * 16 : (q + 1) * 16, cols]
            grads[n, 160:168] = grad_three[:, (q % 2) * LANES : (q % 2 + 1) * LANES]
        back[b] = dot(w_one[e, :LAT], delta_one).astype(bf16)


def texels_kernel(half, back_a, back_b, preds_a, preds_b, index_a, index_b, out):
    acc = jnp.zeros((GROUPS * LAT, 256), f32)
    for rows_back, index in ((back_a, index_a), (back_b, index_b)):
        for b in range(2):
            rows = index[b]
            group = rows[3:4].astype(jnp.int32)
            low_hot = hot(rows[4:5].astype(jnp.int32), 256)
            grad = rows_back[b].astype(f32)
            spread = [jnp.where(group == r + 1, grad, 0.0).astype(bf16) for r in range(GROUPS)]
            acc = acc + dot_nt(jnp.concatenate(spread, axis=0), low_hot)
    for b in range(8):
        for s in range(2):
            out[2 * b + s, :TEX_ROWS] = acc[b * TEX_ROWS : (b + 1) * TEX_ROWS, s * LANES : (s + 1) * LANES].astype(bf16)
    left = iota((8, LANES), 1) < CAP
    keep = half[0]
    for j in range(N_EXP // 2):
        cols = slice(j * LANES, (j + 1) * LANES)
        low, high = [], []
        for h in range(2):
            one = jnp.where(keep == h, preds_b[0, :, cols], preds_a[0, :, cols])
            two = jnp.where(keep == h, preds_b[1, :, cols], preds_a[1, :, cols])
            low.append(jnp.where(left, one, pltpu.roll(two, CAP, 1)))
            high.append(jnp.where(left, pltpu.roll(one, CAP, 1), two))
        out[2 * j, TEX_ROWS:] = jnp.concatenate(low, axis=0).astype(bf16)
        out[2 * j + 1, TEX_ROWS:] = jnp.concatenate(high, axis=0).astype(bf16)


def finish_kernel(got, slot, latents, mean, square, new_latents, new_mean, new_square, predictions):
    texel_grad = jnp.zeros((TEX_ROWS, LANES), f32)
    for j in range(N_EXP):
        texel_grad = texel_grad + got[j, :TEX_ROWS].astype(f32)
    next_mean = decay_one * mean[...] + (1.0 - decay_one) * texel_grad
    next_square = decay_two * square[...] + (1.0 - decay_two) * texel_grad * texel_grad
    new_mean[...] = next_mean
    new_square[...] = next_square
    new_latents[...] = latents[...] - step_rate * next_mean / (jnp.sqrt(next_square) + epsilon)
    table = jnp.concatenate([got[j, TEX_ROWS:] for j in range(N_EXP)], axis=0)
    place = slot[...]
    lane = place & (LANES - 1)
    pair = place >> 7
    for i in range(CHUNKS):
        row = slice(i, i + 1)
        picked = dot(table, hot(lane[row], LANES))
        total = jnp.zeros((8, LANES), f32)
        for g in range(32):
            total = total + jnp.where(pair[row] == g, picked[g * 8 : (g + 1) * 8], 0.0)
        predictions[:, i * LANES : (i + 1) * LANES] = total[:OUTC]


def unpack_kernel(packed, grad_one, grad_two, grad_three):
    for e in range(4):
        for q in range(4):
            n = 2 * (4 * (e % 2) + q) + e // 2
            for s in range(2):
                cols = slice(s * LANES, (s + 1) * LANES)
                grad_two[e, q * 64 : (q + 1) * 64, cols] = packed[n, s * 64 : (s + 1) * 64].astype(f32)
                grad_one[e, q * 16 : (q + 1) * 16, cols] = packed[n, 128 + s * 16 : 128 + (s + 1) * 16].astype(f32)
            if q < 2:
                for c in range(OUTC):
                    grad_three[c, e : e + 1, q * LANES : (q + 1) * LANES] = packed[n, 160:168].astype(f32)[c : c + 1]


def call(kernel, outs, scratch=(), in_specs=None, flops=0):
    more = {} if in_specs is None else {"in_specs": in_specs}
    cost = pl.CostEstimate(flops=flops, transcendentals=0, bytes_accessed=0) if flops else None
    return pl.pallas_call(
        kernel,
        out_shape=outs,
        scratch_shapes=list(scratch),
        compiler_params=pltpu.CompilerParams(vmem_limit_bytes=48 << 20),
        cost_estimate=cost,
        **more,
    )


def shape(dims, kind=f32):
    return jax.ShapeDtypeStruct(dims, kind)


def on_device(
    latents,
    latent_mean,
    latent_square,
    weight_one,
    weight_two,
    weight_three,
    dir_table,
    materials,
    tile_ids,
    texel_ids,
    dir_ids,
    targets,
):
    flat = lambda a: a.reshape(TEX_ROWS, LANES)
    rows = lambda a: a.reshape(CHUNKS, LANES)
    hbm = pl.BlockSpec(memory_space=pltpu.HBM)
    vmem = pl.BlockSpec(memory_space=pltpu.VMEM)
    smem = pl.BlockSpec(memory_space=pltpu.SMEM)
    index_rows = pltpu.VMEM((CHUNKS, LANES), jnp.int32)
    send, slot = call(
        route_kernel,
        (shape((N_EXP, SEND_ROWS, LANES), bf16), shape((CHUNKS, LANES), jnp.int32)),
        [index_rows] * 4
        + [pltpu.VMEM((OUTC, ROWS), f32), pltpu.VMEM((TEX_ROWS, LANES), f32), pltpu.SemaphoreType.DMA((6,))],
        [hbm] * 6,
    )(*[
        pltpu.with_memory_space_constraint(a, pltpu.HBM)
        for a in (rows(materials), rows(tile_ids), rows(texel_ids), rows(dir_ids), targets, flat(latents))
    ])
    recv = lax.all_to_all(send, "exp", 0, 0, tiled=True)
    three = jnp.pad(weight_three, ((0, 0), (0, 8 - OUTC), (0, 0)))
    weights = (
        weight_one,
        jnp.swapaxes(weight_one, 1, 2),
        weight_two,
        jnp.swapaxes(weight_two, 1, 2),
        three,
        jnp.swapaxes(three, 1, 2),
        dir_table.T,
    )
    core = (lax.axis_index("rep") % 2).astype(jnp.int32).reshape(1)
    half = lambda kind: call(
        half_kernel,
        (
            shape((N_REP // 2, GRAD_ROWS, LANES), kind),
            shape((2, LAT, SLOTS), bf16),
            shape((2, 8, SLOTS)),
            shape((2, 8, SLOTS)),
        ),
        [pltpu.VMEM((GROUPS * LAT, 256), bf16)],
        [smem] + [vmem] * 8,
        2000000000,
    )
    grads_a, back_a, preds_a, index_a = half(bf16)(1 - core, recv, *weights)
    from_core = lax.ppermute(grads_a, "rep", [(i, i ^ 1) for i in range(N_REP)])
    grads_b, back_b, preds_b, index_b = half(f32)(core, recv, *weights)
    chip = (grads_b + from_core.astype(f32)).astype(bf16)
    chips = [list(range(c, N_REP, 2)) for c in range(2)]
    parts = lax.all_to_all(chip, "rep", 0, 0, tiled=True, axis_index_groups=chips)
    back = call(
        texels_kernel,
        shape((N_EXP, SEND_ROWS, LANES), bf16),
        (),
        [smem] + [vmem] * 6,
        2000000000,
    )(core, back_a, back_b, preds_a, preds_b, index_a, index_b)
    own = jnp.sum(parts.astype(f32), axis=0).astype(bf16)
    back, own = lax.optimization_barrier((back, own))
    got = lax.all_to_all(back, "exp", 0, 0, tiled=True)
    packed = lax.all_gather(own, "rep", axis=0, tiled=False)
    new_latents, new_mean, new_square, predictions = call(
        finish_kernel,
        (shape((TEX_ROWS, LANES)), shape((TEX_ROWS, LANES)), shape((TEX_ROWS, LANES)), shape((OUTC, ROWS))),
    )(got, slot, flat(latents), flat(latent_mean), flat(latent_square))
    grad_one, grad_two, grad_three = call(
        unpack_kernel,
        (shape(weight_one.shape), shape(weight_two.shape), shape((OUTC, 4, HID))),
    )(packed)
    grad_three = jnp.swapaxes(grad_three, 0, 1)
    whole = lambda a: a.reshape(latents.shape)
    return (
        whole(new_latents),
        whole(new_mean),
        whole(new_square),
        predictions,
        grad_one,
        grad_two,
        grad_three,
    )


def solution(mesh):
    in_specs = (
        P("rep", None, "exp"),
        P("rep", None, "exp"),
        P("rep", None, "exp"),
        P("exp", None, None),
        P("exp", None, None),
        P("exp", None, None),
        P(),
        P(("rep", "exp"), None),
        P(("rep", "exp")),
        P(("rep", "exp")),
        P(("rep", "exp")),
        P(None, ("rep", "exp")),
    )
    out_specs = (
        P("rep", None, "exp"),
        P("rep", None, "exp"),
        P("rep", None, "exp"),
        P(None, ("rep", "exp")),
        P("exp", None, None),
        P("exp", None, None),
        P("exp", None, None),
    )
    return jax.shard_map(on_device, mesh=mesh, in_specs=in_specs, out_specs=out_specs, check_vma=False)
```

```python
import jax
import jax.numpy as jnp
from jax import lax
from jax.experimental import pallas as pl
from jax.experimental.pallas import tpu as pltpu
from jax.sharding import PartitionSpec as P

LAT = 32
HID = 256
OUTC = 3
LANES = 128
N_EXP = 16
N_REP = 16
CAP = 64
ROWS = 2048
CHUNKS = ROWS // LANES
SLOTS = N_EXP * CAP
GROUPS = 8
LOW = 512
PIECES = 2
TEX_ROWS = 64
SEND_ROWS = TEX_ROWS + 16
GRAD_ROWS = 168

decay_one = 0.9
decay_two = 0.99
step_rate = 0.05
epsilon = 1e-08

f32 = jnp.float32
bf16 = jnp.bfloat16


def dot(a, b):
    return jnp.dot(a, b, preferred_element_type=f32)


def dot_nt(a, b):
    return lax.dot_general(a, b, (((1,), (1,)), ((), ())), preferred_element_type=f32)


def iota(shape, dim):
    return lax.broadcasted_iota(jnp.int32, shape, dim)


def hot(index, count, start=0):
    same = iota((count, index.shape[1]), 0) + start == index
    return jnp.where(same, 1.0, 0.0).astype(bf16)


def hot_wide(keys, start=0):
    column = (iota((256, LANES), 0) + start).astype(bf16)
    spread = jnp.broadcast_to(keys.astype(bf16), (256, keys.shape[1]))
    parts = [
        jnp.where(column == spread[:, i : i + LANES], jnp.ones((), bf16), jnp.zeros((), bf16))
        for i in range(0, keys.shape[1], LANES)
    ]
    return jnp.concatenate(parts, axis=1)


def split_index(rows):
    high = rows[3:4].astype(jnp.int32) - 1
    group = high >> 1
    bit = high & 1
    low = jnp.concatenate([hot_wide(jnp.where(bit == b, rows[4:5], -1.0)) for b in range(2)], axis=0)
    return group, low


def route_kernel(mat, tile_in, texel_in, direction_in, targets_in, latents_in, send, slot, *scratch):
    material_in, tile, texel, direction, targets, latents, sems = scratch
    copies = [
        pltpu.make_async_copy(source, target, sems.at[n])
        for n, (source, target) in enumerate(
            [
                (mat, material_in),
                (tile_in, tile),
                (texel_in, texel),
                (direction_in, direction),
                (targets_in, targets),
                (latents_in, latents),
            ]
        )
    ]
    for copy in copies:
        copy.start()
    for copy in copies:
        copy.wait()
    material = material_in[...]
    hots = [hot(material[i : i + 1], 64) for i in range(CHUNKS)]
    upper = jnp.where(iota((LANES, LANES), 0) <= iota((LANES, LANES), 1), 1.0, 0.0).astype(bf16)
    counted = dot(jnp.concatenate(hots, axis=0), upper)
    before = jnp.zeros((64, 1), f32)
    places = []
    for i in range(CHUNKS):
        here = counted[i * 64 : (i + 1) * 64]
        places.append(jnp.sum(hots[i].astype(f32) * (here + before), axis=0, keepdims=True))
        before = before + here[:, LANES - 1 :]
    place = jnp.concatenate(places, axis=0).astype(jnp.int32) - 1
    lane = (material & 1) * CAP + place
    pair = material >> 1
    slot[...] = pair * LANES + lane
    texels = texel[...]
    group = (texels >> 9) * 2 + tile[...]
    high = (group * 2 + ((texels >> 8) & 1) + 1).astype(f32)
    low = (texels & 255).astype(f32)
    heading = (direction[...] + 1).astype(f32)
    values = []
    lanes_hot = []
    for i in range(CHUNKS):
        row = slice(i, i + 1)
        val = jnp.concatenate(
            [
                targets[:, i * LANES : (i + 1) * LANES],
                high[row],
                low[row],
                heading[row],
                jnp.zeros((2, LANES), f32),
            ],
            axis=0,
        )
        parts = [jnp.where(pair[row] == g, val, 0.0) for g in range(32)]
        values.append(jnp.concatenate(parts, axis=0).astype(bf16))
        lanes_hot.append(hot(lane[row], LANES))
    out = dot_nt(jnp.concatenate(values, axis=1), jnp.concatenate(lanes_hot, axis=1)).astype(bf16)
    own = latents[...].astype(bf16)
    for j in range(N_EXP):
        send[j, :TEX_ROWS] = own
        send[j, TEX_ROWS:] = out[j * 16 : (j + 1) * 16]


def half_kernel(
    half, recv, w_one, w_one_t, w_two, w_two_t, w_three, w_three_t, dir_t, grads, back, preds, index, tex
):
    h = half[0]
    for b in range(4):
        for s in range(4):
            tex[b * TEX_ROWS : (b + 1) * TEX_ROWS, s * LANES : (s + 1) * LANES] = recv[4 * b + s, :TEX_ROWS]
    left = iota((8, LANES), 1) < CAP
    sides = ([], [])
    for j in range(N_EXP // 2):
        both = [recv[2 * j + s, TEX_ROWS:].astype(f32) for s in range(2)]
        first, second = [jnp.where(h == 0, v[:8], v[8:]) for v in both]
        sides[0].append(jnp.where(left, first, pltpu.roll(second, CAP, 1)))
        sides[1].append(jnp.where(left, pltpu.roll(first, CAP, 1), second))
    units = [(b, c) for b in range(2) for c in range(PIECES)]
    width = SLOTS // PIECES
    full = [jnp.concatenate(side, axis=1) for side in sides]
    for b in range(2):
        index[b] = full[b]
    rows = {(b, c): full[b][:, c * width : (c + 1) * width] for b, c in units}
    split = {n: split_index(rows[n]) for n in units}
    picked = {n: dot(tex[...], split[n][1]).reshape(GROUPS, LAT // 8, 8, width) for n in units}
    heading = {n: dot(dir_t[...], hot_wide(rows[n][5:6], 1)) for n in units}
    x = {}
    for n in units:
        wide = jnp.broadcast_to(split[n][0], (8, width))
        lat = jnp.where((wide == 0)[None], picked[n][0], 0.0)
        for r in range(1, GROUPS):
            lat = jnp.where((wide == r)[None], picked[n][r], lat)
        x[n] = jnp.concatenate([lat.reshape(LAT, width), heading[n]], axis=0).astype(bf16)
    act_one, slope_one, act_two, slope_two, misfit, delta_two, delta_one = ({} for _ in range(7))
    u = {n: dot(w_one_t[2 * h + n[0]], x[n]) for n in units}
    for n in units:
        t = jnp.tanh(u[n])
        act_one[n] = (u[n] * (1.0 + t)).astype(bf16)
        slope_one[n] = (1.0 + t) * (1.0 + u[n] * (1.0 - t))
    u = {n: dot(w_two_t[2 * h + n[0]], act_one[n]) for n in units}
    for n in units:
        t = jnp.tanh(u[n])
        act_two[n] = (u[n] * (1.0 + t)).astype(bf16)
        slope_two[n] = (1.0 + t) * (1.0 + u[n] * (1.0 - t))
    for n in units:
        b, c = n
        pred = dot(w_three[2 * h + b], act_two[n])
        preds[b, :, c * width : (c + 1) * width] = pred
        misfit[n] = jnp.where(iota((8, width), 0) < OUTC, pred - rows[n], 0.0).astype(bf16)
    half_back = {n: dot(w_three_t[2 * h + n[0]], misfit[n]) for n in units}
    for n in units:
        delta_two[n] = (half_back[n] * slope_two[n]).astype(bf16)
    half_back = {n: dot(w_two[2 * h + n[0]], delta_two[n]) for n in units}
    for b in range(2):
        pieces = [(b, c) for c in range(PIECES)]
        grad_two = sum(dot_nt(act_one[n], delta_two[n]) for n in pieces).astype(grads.dtype)
        grad_three = sum(dot_nt(misfit[n], act_two[n]) for n in pieces).astype(grads.dtype)
        for q in range(4):
            for s in range(2):
                grads[4 * b + q, s * 64 : (s + 1) * 64] = grad_two[q * 64 : (q + 1) * 64, s * LANES : (s + 1) * LANES]
            grads[4 * b + q, 160:168] = grad_three[:, (q % 2) * LANES : (q % 2 + 1) * LANES]
    for n in units:
        delta_one[n] = (half_back[n] * slope_one[n]).astype(bf16)
    for b in range(2):
        pieces = [(b, c) for c in range(PIECES)]
        grad_one = sum(dot_nt(x[n], delta_one[n]) for n in pieces).astype(grads.dtype)
        for q in range(4):
            for s in range(2):
                grads[4 * b + q, 128 + s * 16 : 128 + (s + 1) * 16] = grad_one[
                    q * 16 : (q + 1) * 16, s * LANES : (s + 1) * LANES
                ]
    for n in units:
        b, c = n
        back[b, :, c * width : (c + 1) * width] = dot(w_one[2 * h + b, :LAT], delta_one[n]).astype(bf16)


def texels_kernel(half, back_a, back_b, preds_a, preds_b, index_a, index_b, out):
    acc = jnp.zeros((GROUPS * LAT, LOW), f32)
    for rows_back, index in ((back_a, index_a), (back_b, index_b)):
        for b in range(2):
            rows = index[b]
            group, low_hot = split_index(rows)
            wide = jnp.broadcast_to(group.astype(bf16), (16, SLOTS))
            grad = rows_back[b].reshape(LAT // 16, 16, SLOTS)
            spread = [
                jnp.where((wide == jnp.array(r, bf16))[None], grad, jnp.zeros((), bf16)).reshape(LAT, SLOTS)
                for r in range(GROUPS)
            ]
            acc = acc + dot_nt(jnp.concatenate(spread, axis=0), low_hot)
    for b in range(4):
        for s in range(4):
            out[4 * b + s, :TEX_ROWS] = acc[b * TEX_ROWS : (b + 1) * TEX_ROWS, s * LANES : (s + 1) * LANES].astype(bf16)
    left = iota((8, LANES), 1) < CAP
    keep = half[0]
    for j in range(N_EXP // 2):
        cols = slice(j * LANES, (j + 1) * LANES)
        low, high = [], []
        for h in range(2):
            one = jnp.where(keep == h, preds_b[0, :, cols], preds_a[0, :, cols])
            two = jnp.where(keep == h, preds_b[1, :, cols], preds_a[1, :, cols])
            low.append(jnp.where(left, one, pltpu.roll(two, CAP, 1)))
            high.append(jnp.where(left, pltpu.roll(one, CAP, 1), two))
        out[2 * j, TEX_ROWS:] = jnp.concatenate(low, axis=0).astype(bf16)
        out[2 * j + 1, TEX_ROWS:] = jnp.concatenate(high, axis=0).astype(bf16)


def finish_kernel(
    packed, got, slot, latents, mean, square, out_one, out_two, out_three, out_latents, out_mean, out_square, out_pred, *scratch
):
    grad_one, grad_two, grad_three, new_latents, new_mean, new_square, predictions, sems = scratch
    copies = []

    def leave(source, target):
        copies.append(pltpu.make_async_copy(source, target, sems.at[len(copies)]))
        copies[-1].start()

    for e in range(4):
        for q in range(4):
            n = 2 * (4 * (e % 2) + q) + e // 2
            for s in range(2):
                cols = slice(s * LANES, (s + 1) * LANES)
                grad_two[e, q * 64 : (q + 1) * 64, cols] = packed[n, s * 64 : (s + 1) * 64].astype(f32)
                grad_one[e, q * 16 : (q + 1) * 16, cols] = packed[n, 128 + s * 16 : 128 + (s + 1) * 16].astype(f32)
            if q < 2:
                for c in range(OUTC):
                    grad_three[c, e : e + 1, q * LANES : (q + 1) * LANES] = packed[n, 160:168].astype(f32)[c : c + 1]
        leave(grad_two.at[e], out_two.at[e])
    leave(grad_one, out_one)
    leave(grad_three, out_three)
    texel_grad = jnp.zeros((TEX_ROWS, LANES), f32)
    for j in range(N_EXP):
        texel_grad = texel_grad + got[j, :TEX_ROWS].astype(f32)
    next_mean = decay_one * mean[...] + (1.0 - decay_one) * texel_grad
    next_square = decay_two * square[...] + (1.0 - decay_two) * texel_grad * texel_grad
    new_mean[...] = next_mean
    new_square[...] = next_square
    new_latents[...] = latents[...] - step_rate * next_mean / (jnp.sqrt(next_square) + epsilon)
    leave(new_mean, out_mean)
    leave(new_square, out_square)
    leave(new_latents, out_latents)
    table = jnp.concatenate([got[j, TEX_ROWS:] for j in range(N_EXP)], axis=0)
    place = slot[...]
    lane = place & (LANES - 1)
    pair = place >> 7
    for i in range(CHUNKS):
        row = slice(i, i + 1)
        picked = dot(table, hot(lane[row], LANES))
        wide = jnp.broadcast_to(pair[row], (8, LANES))
        total = jnp.where(wide == 0, picked[:8], 0.0)
        for g in range(1, 32):
            total = jnp.where(wide == g, picked[g * 8 : (g + 1) * 8], total)
        predictions[:, i * LANES : (i + 1) * LANES] = total[:OUTC]
    leave(predictions, out_pred)
    for copy in copies:
        copy.wait()


def call(kernel, outs, scratch=(), in_specs=None, flops=0, out_specs=None):
    more = {} if in_specs is None else {"in_specs": in_specs}
    if out_specs is not None:
        more["out_specs"] = out_specs
    cost = pl.CostEstimate(flops=flops, transcendentals=0, bytes_accessed=0) if flops else None
    return pl.pallas_call(
        kernel,
        out_shape=outs,
        scratch_shapes=list(scratch),
        compiler_params=pltpu.CompilerParams(vmem_limit_bytes=48 << 20),
        cost_estimate=cost,
        **more,
    )


def shape(dims, kind=f32):
    return jax.ShapeDtypeStruct(dims, kind)


def on_device(
    latents,
    latent_mean,
    latent_square,
    weight_one,
    weight_two,
    weight_three,
    dir_table,
    materials,
    tile_ids,
    texel_ids,
    dir_ids,
    targets,
):
    flat = lambda a: a.reshape(TEX_ROWS, LANES)
    rows = lambda a: a.reshape(CHUNKS, LANES)
    hbm = pl.BlockSpec(memory_space=pltpu.HBM)
    vmem = pl.BlockSpec(memory_space=pltpu.VMEM)
    smem = pl.BlockSpec(memory_space=pltpu.SMEM)
    index_rows = pltpu.VMEM((CHUNKS, LANES), jnp.int32)
    send, slot = call(
        route_kernel,
        (shape((N_EXP, SEND_ROWS, LANES), bf16), shape((CHUNKS, LANES), jnp.int32)),
        [index_rows] * 4
        + [pltpu.VMEM((OUTC, ROWS), f32), pltpu.VMEM((TEX_ROWS, LANES), f32), pltpu.SemaphoreType.DMA((6,))],
        [hbm] * 6,
    )(*[
        pltpu.with_memory_space_constraint(a, pltpu.HBM)
        for a in (rows(materials), rows(tile_ids), rows(texel_ids), rows(dir_ids), targets, flat(latents))
    ])
    recv = lax.all_to_all(send, "exp", 0, 0, tiled=True)
    three = jnp.pad(weight_three, ((0, 0), (0, 8 - OUTC), (0, 0)))
    weights = (
        weight_one,
        jnp.swapaxes(weight_one, 1, 2) * 0.5,
        weight_two * 0.5,
        jnp.swapaxes(weight_two, 1, 2) * 0.5,
        three,
        jnp.swapaxes(three, 1, 2) * 0.5,
        dir_table.T,
    )
    core = (lax.axis_index("rep") % 2).astype(jnp.int32).reshape(1)
    half = lambda kind: call(
        half_kernel,
        (
            shape((N_REP // 2, GRAD_ROWS, LANES), kind),
            shape((2, LAT, SLOTS), bf16),
            shape((2, 8, SLOTS)),
            shape((2, 8, SLOTS)),
        ),
        [pltpu.VMEM((GROUPS * LAT, LOW), bf16)],
        [smem] + [vmem] * 8,
        2000000000,
    )
    grads_a, back_a, preds_a, index_a = half(bf16)(1 - core, recv, *weights)
    from_core = lax.ppermute(grads_a, "rep", [(i, i ^ 1) for i in range(N_REP)])
    grads_b, back_b, preds_b, index_b = half(f32)(core, recv, *weights)
    chip = (grads_b + from_core.astype(f32)).astype(bf16)
    chips = [list(range(c, N_REP, 2)) for c in range(2)]
    parts = lax.all_to_all(chip, "rep", 0, 0, tiled=True, axis_index_groups=chips)
    back = call(
        texels_kernel,
        shape((N_EXP, SEND_ROWS, LANES), bf16),
        (),
        [smem] + [vmem] * 6,
        2000000000,
    )(core, back_a, back_b, preds_a, preds_b, index_a, index_b)
    own = jnp.sum(parts.astype(f32), axis=0).astype(bf16)
    back, own = lax.optimization_barrier((back, own))
    got = lax.all_to_all(back, "exp", 0, 0, tiled=True)
    packed = lax.all_gather(own, "rep", axis=0, tiled=False)
    plane = (TEX_ROWS, LANES)
    outs = (weight_one.shape, weight_two.shape, (OUTC, 4, HID), plane, plane, plane, (OUTC, ROWS))
    grad_one, grad_two, grad_three, new_latents, new_mean, new_square, predictions = call(
        finish_kernel,
        tuple(shape(dims) for dims in outs),
        [pltpu.VMEM(dims, f32) for dims in outs] + [pltpu.SemaphoreType.DMA((10,))],
        [vmem] * 6,
        0,
        tuple([hbm] * 7),
    )(packed, got, slot, flat(latents), flat(latent_mean), flat(latent_square))
    grad_three = jnp.swapaxes(grad_three, 0, 1)
    whole = lambda a: a.reshape(latents.shape)
    return (
        whole(new_latents),
        whole(new_mean),
        whole(new_square),
        predictions,
        grad_one,
        grad_two,
        grad_three,
    )


def solution(mesh):
    in_specs = (
        P("rep", None, "exp"),
        P("rep", None, "exp"),
        P("rep", None, "exp"),
        P("exp", None, None),
        P("exp", None, None),
        P("exp", None, None),
        P(),
        P(("rep", "exp"), None),
        P(("rep", "exp")),
        P(("rep", "exp")),
        P(("rep", "exp")),
        P(None, ("rep", "exp")),
    )
    out_specs = (
        P("rep", None, "exp"),
        P("rep", None, "exp"),
        P("rep", None, "exp"),
        P(None, ("rep", "exp")),
        P("exp", None, None),
        P("exp", None, None),
        P("exp", None, None),
    )
    return jax.shard_map(on_device, mesh=mesh, in_specs=in_specs, out_specs=out_specs, check_vma=False)
```

```python
import jax
import jax.numpy as jnp
from jax import lax
from jax.experimental import pallas as pl
from jax.experimental.pallas import tpu as pltpu
from jax.sharding import PartitionSpec as P

LAT = 32
HID = 256
OUTC = 3
LANES = 128
N_EXP = 16
N_REP = 16
CAP = 64
ROWS = 2048
CHUNKS = ROWS // LANES
SLOTS = N_EXP * CAP
GROUPS = 8
LOW = 512
PIECES = 2
TEX_ROWS = 64
SEND_ROWS = TEX_ROWS + 16
GRAD_ROWS = 168

decay_one = 0.9
decay_two = 0.99
step_rate = 0.05
epsilon = 1e-08

f32 = jnp.float32
bf16 = jnp.bfloat16


def dot(a, b):
    return jnp.dot(a, b, preferred_element_type=f32)


def dot_nt(a, b):
    return lax.dot_general(a, b, (((1,), (1,)), ((), ())), preferred_element_type=f32)


def iota(shape, dim):
    return lax.broadcasted_iota(jnp.int32, shape, dim)


def hot(index, count, start=0):
    same = iota((count, index.shape[1]), 0) + start == index
    return jnp.where(same, 1.0, 0.0).astype(bf16)


def hot_wide(keys, start=0):
    column = (iota((256, LANES), 0) + start).astype(bf16)
    spread = jnp.broadcast_to(keys.astype(bf16), (256, keys.shape[1]))
    parts = [
        jnp.where(column == spread[:, i : i + LANES], jnp.ones((), bf16), jnp.zeros((), bf16))
        for i in range(0, keys.shape[1], LANES)
    ]
    return jnp.concatenate(parts, axis=1)


def split_index(rows):
    high = rows[3:4].astype(jnp.int32) - 1
    group = high >> 1
    bit = high & 1
    low = jnp.concatenate([hot_wide(jnp.where(bit == b, rows[4:5], -1.0)) for b in range(2)], axis=0)
    return group, low


def route_kernel(mat, tile_in, texel_in, direction_in, targets_in, latents_in, send, slot, *scratch):
    material_in, tile, texel, direction, targets, latents, own, packets, sems = scratch
    copies = [
        pltpu.make_async_copy(source, target, sems.at[n])
        for n, (source, target) in enumerate(
            [
                (mat, material_in),
                (tile_in, tile),
                (texel_in, texel),
                (direction_in, direction),
                (targets_in, targets),
                (latents_in, latents),
            ]
        )
    ]
    for copy in reversed(copies):
        copy.start()
    copies[5].wait()
    own[...] = latents[...].astype(bf16)
    leaving = [
        pltpu.make_async_copy(own, send.at[j, pl.ds(0, TEX_ROWS)], sems.at[6 + j]) for j in range(N_EXP)
    ]
    for copy in leaving:
        copy.start()
    for copy in copies[:5]:
        copy.wait()
    material = material_in[...]
    hots = [hot(material[i : i + 1], 64) for i in range(CHUNKS)]
    upper = jnp.where(iota((LANES, LANES), 0) <= iota((LANES, LANES), 1), 1.0, 0.0).astype(bf16)
    counted = dot(jnp.concatenate(hots, axis=0), upper)
    before = jnp.zeros((64, 1), f32)
    places = []
    for i in range(CHUNKS):
        here = counted[i * 64 : (i + 1) * 64]
        places.append(jnp.sum(hots[i].astype(f32) * (here + before), axis=0, keepdims=True))
        before = before + here[:, LANES - 1 :]
    place = jnp.concatenate(places, axis=0).astype(jnp.int32) - 1
    lane = (material & 1) * CAP + place
    pair = material >> 1
    slot[...] = pair * LANES + lane
    texels = texel[...]
    group = (texels >> 9) * 2 + tile[...]
    high = (group * 2 + ((texels >> 8) & 1) + 1).astype(f32)
    low = (texels & 255).astype(f32)
    heading = (direction[...] + 1).astype(f32)
    values = []
    lanes_hot = []
    for i in range(CHUNKS):
        row = slice(i, i + 1)
        val = jnp.concatenate(
            [
                targets[:, i * LANES : (i + 1) * LANES],
                high[row],
                low[row],
                heading[row],
                jnp.zeros((2, LANES), f32),
            ],
            axis=0,
        )
        parts = [jnp.where(pair[row] == g, val, 0.0) for g in range(32)]
        values.append(jnp.concatenate(parts, axis=0).astype(bf16))
        lanes_hot.append(hot(lane[row], LANES))
    out = dot_nt(jnp.concatenate(values, axis=1), jnp.concatenate(lanes_hot, axis=1)).astype(bf16)
    for j in range(N_EXP):
        packets[j] = out[j * 16 : (j + 1) * 16]
    last = pltpu.make_async_copy(packets, send.at[:, pl.ds(TEX_ROWS, 16)], sems.at[6 + N_EXP])
    last.start()
    for copy in leaving:
        copy.wait()
    last.wait()


def put(grads, n, rows, value, more):
    if more is not None:
        value = value + more[n, rows].astype(f32)
    grads[n, rows] = value.astype(bf16)


def put_two(grads, b, value, more=None):
    for q in range(4):
        for s in range(2):
            part = value[q * 64 : (q + 1) * 64, s * LANES : (s + 1) * LANES]
            put(grads, 4 * b + q, slice(s * 64, (s + 1) * 64), part, more)


def put_one(grads, b, value, more=None):
    for q in range(4):
        for s in range(2):
            part = value[q * 16 : (q + 1) * 16, s * LANES : (s + 1) * LANES]
            put(grads, 4 * b + q, slice(128 + s * 16, 128 + (s + 1) * 16), part, more)


def put_three(grads, b, value, more=None):
    for q in range(4):
        part = value[:, (q % 2) * LANES : (q % 2 + 1) * LANES]
        put(grads, 4 * b + q, slice(160, 168), part, more)


def half_kernel(half, recv, w_one, w_one_t, w_two, w_two_t, w_three, w_three_t, dir_t, back, preds, index, *rest):
    h = half[0]
    tex = rest[-1]
    for b in range(4):
        for s in range(4):
            tex[b * TEX_ROWS : (b + 1) * TEX_ROWS, s * LANES : (s + 1) * LANES] = recv[4 * b + s, :TEX_ROWS]
    left = iota((8, LANES), 1) < CAP
    sides = ([], [])
    for j in range(N_EXP // 2):
        both = [recv[2 * j + s, TEX_ROWS:].astype(f32) for s in range(2)]
        first, second = [jnp.where(h == 0, v[:8], v[8:]) for v in both]
        sides[0].append(jnp.where(left, first, pltpu.roll(second, CAP, 1)))
        sides[1].append(jnp.where(left, pltpu.roll(first, CAP, 1), second))
    units = [(b, c) for b in range(2) for c in range(PIECES)]
    width = SLOTS // PIECES
    full = [jnp.concatenate(side, axis=1) for side in sides]
    for b in range(2):
        index[b] = full[b]
    rows = {(b, c): full[b][:, c * width : (c + 1) * width] for b, c in units}
    split = {n: split_index(rows[n]) for n in units}
    picked = {n: dot(tex[...], split[n][1]).reshape(GROUPS, LAT // 8, 8, width) for n in units}
    heading = {n: dot(dir_t[...], hot_wide(rows[n][5:6], 1)) for n in units}
    x = {}
    for n in units:
        wide = jnp.broadcast_to(split[n][0], (8, width))
        lat = jnp.where((wide == 0)[None], picked[n][0], 0.0)
        for r in range(1, GROUPS):
            lat = jnp.where((wide == r)[None], picked[n][r], lat)
        x[n] = jnp.concatenate([lat.reshape(LAT, width), heading[n]], axis=0).astype(bf16)
    act_one, slope_one, act_two, slope_two, misfit, delta_two, delta_one = ({} for _ in range(7))
    u = {n: dot(w_one_t[2 * h + n[0]], x[n]) for n in units}
    for n in units:
        t = jnp.tanh(u[n])
        act_one[n] = (u[n] * (1.0 + t)).astype(bf16)
        slope_one[n] = (1.0 + t) * (1.0 + u[n] * (1.0 - t))
    u = {n: dot(w_two_t[2 * h + n[0]], act_one[n]) for n in units}
    for n in units:
        t = jnp.tanh(u[n])
        act_two[n] = (u[n] * (1.0 + t)).astype(bf16)
        slope_two[n] = (1.0 + t) * (1.0 + u[n] * (1.0 - t))
    for n in units:
        b, c = n
        pred = dot(w_three[2 * h + b], act_two[n])
        preds[b, :, c * width : (c + 1) * width] = pred
        misfit[n] = jnp.where(iota((8, width), 0) < OUTC, pred - rows[n], 0.0).astype(bf16)
    half_back = {n: dot(w_three_t[2 * h + n[0]], misfit[n]) for n in units}
    for n in units:
        delta_two[n] = (half_back[n] * slope_two[n]).astype(bf16)
    half_back = {n: dot(w_two[2 * h + n[0]], delta_two[n]) for n in units}
    if len(rest) == 2:
        for b in range(2):
            pieces = [(b, c) for c in range(PIECES)]
            put_two(rest[0], b, sum(dot_nt(act_one[n], delta_two[n]) for n in pieces))
            put_three(rest[0], b, sum(dot_nt(misfit[n], act_two[n]) for n in pieces))
    else:
        for n in units:
            b, c = n
            kept = (act_one, delta_two, misfit, act_two, x)
            for ref, value in zip(rest[:5], kept):
                ref[b, :, c * width : (c + 1) * width] = value[n]
    for n in units:
        delta_one[n] = (half_back[n] * slope_one[n]).astype(bf16)
    if len(rest) == 2:
        for b in range(2):
            put_one(rest[0], b, sum(dot_nt(x[b, c], delta_one[b, c]) for c in range(PIECES)))
    else:
        for n in units:
            b, c = n
            rest[5][b, :, c * width : (c + 1) * width] = delta_one[n]
    for n in units:
        b, c = n
        back[b, :, c * width : (c + 1) * width] = dot(w_one[2 * h + b, :LAT], delta_one[n]).astype(bf16)


def weights_kernel(act_one, delta_two, misfit, act_two, x, delta_one, from_core, out, grads, sems):
    copies = []
    for b in range(2):
        put_two(grads, b, dot_nt(act_one[b], delta_two[b]), from_core)
        put_one(grads, b, dot_nt(x[b], delta_one[b]), from_core)
        put_three(grads, b, dot_nt(misfit[b], act_two[b]), from_core)
        copies.append(
            pltpu.make_async_copy(grads.at[pl.ds(4 * b, 4)], out.at[pl.ds(4 * b, 4)], sems.at[b])
        )
        copies[-1].start()
    for copy in copies:
        copy.wait()


def texels_kernel(half, back_a, back_b, preds_a, preds_b, index_a, index_b, out):
    acc = jnp.zeros((GROUPS * LAT, LOW), f32)
    for rows_back, index in ((back_a, index_a), (back_b, index_b)):
        for b in range(2):
            rows = index[b]
            group, low_hot = split_index(rows)
            wide = jnp.broadcast_to(group.astype(bf16), (16, SLOTS))
            grad = rows_back[b].reshape(LAT // 16, 16, SLOTS)
            spread = [
                jnp.where((wide == jnp.array(r, bf16))[None], grad, jnp.zeros((), bf16)).reshape(LAT, SLOTS)
                for r in range(GROUPS)
            ]
            acc = acc + dot_nt(jnp.concatenate(spread, axis=0), low_hot)
    for b in range(4):
        for s in range(4):
            out[4 * b + s, :TEX_ROWS] = acc[b * TEX_ROWS : (b + 1) * TEX_ROWS, s * LANES : (s + 1) * LANES].astype(bf16)
    left = iota((8, LANES), 1) < CAP
    keep = half[0]
    for j in range(N_EXP // 2):
        cols = slice(j * LANES, (j + 1) * LANES)
        low, high = [], []
        for h in range(2):
            one = jnp.where(keep == h, preds_b[0, :, cols], preds_a[0, :, cols])
            two = jnp.where(keep == h, preds_b[1, :, cols], preds_a[1, :, cols])
            low.append(jnp.where(left, one, pltpu.roll(two, CAP, 1)))
            high.append(jnp.where(left, pltpu.roll(one, CAP, 1), two))
        out[2 * j, TEX_ROWS:] = jnp.concatenate(low, axis=0).astype(bf16)
        out[2 * j + 1, TEX_ROWS:] = jnp.concatenate(high, axis=0).astype(bf16)


def finish_kernel(
    packed, got, slot, latents, mean, square, out_one, out_two, out_three, out_latents, out_mean, out_square, out_pred, *scratch
):
    grad_one, grad_two, grad_three, new_latents, new_mean, new_square, predictions, sems = scratch
    copies = []

    def leave(source, target):
        copies.append(pltpu.make_async_copy(source, target, sems.at[len(copies)]))
        copies[-1].start()

    for e in range(4):
        for q in range(4):
            n = 2 * (4 * (e % 2) + q) + e // 2
            for s in range(2):
                cols = slice(s * LANES, (s + 1) * LANES)
                grad_two[e, q * 64 : (q + 1) * 64, cols] = packed[n, s * 64 : (s + 1) * 64].astype(f32)
                grad_one[e, q * 16 : (q + 1) * 16, cols] = packed[n, 128 + s * 16 : 128 + (s + 1) * 16].astype(f32)
            if q < 2:
                for c in range(OUTC):
                    grad_three[c, e : e + 1, q * LANES : (q + 1) * LANES] = packed[n, 160:168].astype(f32)[c : c + 1]
        leave(grad_two.at[e], out_two.at[e])
    leave(grad_one, out_one)
    leave(grad_three, out_three)
    texel_grad = jnp.zeros((TEX_ROWS, LANES), f32)
    for j in range(N_EXP):
        texel_grad = texel_grad + got[j, :TEX_ROWS].astype(f32)
    next_mean = decay_one * mean[...] + (1.0 - decay_one) * texel_grad
    next_square = decay_two * square[...] + (1.0 - decay_two) * texel_grad * texel_grad
    new_mean[...] = next_mean
    new_square[...] = next_square
    new_latents[...] = latents[...] - step_rate * next_mean / (jnp.sqrt(next_square) + epsilon)
    leave(new_mean, out_mean)
    leave(new_square, out_square)
    leave(new_latents, out_latents)
    table = jnp.concatenate([got[j, TEX_ROWS:] for j in range(N_EXP)], axis=0)
    place = slot[...]
    lane = place & (LANES - 1)
    pair = place >> 7
    for i in range(CHUNKS):
        row = slice(i, i + 1)
        picked = dot(table, hot(lane[row], LANES))
        wide = jnp.broadcast_to(pair[row], (8, LANES))
        total = jnp.where(wide == 0, picked[:8], 0.0)
        for g in range(1, 32):
            total = jnp.where(wide == g, picked[g * 8 : (g + 1) * 8], total)
        predictions[:, i * LANES : (i + 1) * LANES] = total[:OUTC]
    leave(predictions, out_pred)
    for copy in copies:
        copy.wait()


def call(kernel, outs, scratch=(), in_specs=None, flops=0, out_specs=None):
    more = {} if in_specs is None else {"in_specs": in_specs}
    if out_specs is not None:
        more["out_specs"] = out_specs
    cost = pl.CostEstimate(flops=flops, transcendentals=0, bytes_accessed=0) if flops else None
    return pl.pallas_call(
        kernel,
        out_shape=outs,
        scratch_shapes=list(scratch),
        compiler_params=pltpu.CompilerParams(vmem_limit_bytes=24 << 20),
        cost_estimate=cost,
        **more,
    )


def shape(dims, kind=f32):
    return jax.ShapeDtypeStruct(dims, kind)


def on_device(
    latents,
    latent_mean,
    latent_square,
    weight_one,
    weight_two,
    weight_three,
    dir_table,
    materials,
    tile_ids,
    texel_ids,
    dir_ids,
    targets,
):
    flat = lambda a: a.reshape(TEX_ROWS, LANES)
    rows = lambda a: a.reshape(CHUNKS, LANES)
    hbm = pl.BlockSpec(memory_space=pltpu.HBM)
    vmem = pl.BlockSpec(memory_space=pltpu.VMEM)
    smem = pl.BlockSpec(memory_space=pltpu.SMEM)
    index_rows = pltpu.VMEM((CHUNKS, LANES), jnp.int32)
    send, slot = call(
        route_kernel,
        (shape((N_EXP, SEND_ROWS, LANES), bf16), shape((CHUNKS, LANES), jnp.int32)),
        [index_rows] * 4
        + [
            pltpu.VMEM((OUTC, ROWS), f32),
            pltpu.VMEM((TEX_ROWS, LANES), f32),
            pltpu.VMEM((TEX_ROWS, LANES), bf16),
            pltpu.VMEM((N_EXP, 16, LANES), bf16),
            pltpu.SemaphoreType.DMA((7 + N_EXP,)),
        ],
        [hbm] * 6,
        0,
        (hbm, vmem),
    )(*[
        pltpu.with_memory_space_constraint(a, pltpu.HBM)
        for a in (rows(materials), rows(tile_ids), rows(texel_ids), rows(dir_ids), targets, flat(latents))
    ])
    recv = lax.all_to_all(send, "exp", 0, 0, tiled=True)
    three = jnp.pad(weight_three, ((0, 0), (0, 8 - OUTC), (0, 0)))
    weights = (
        weight_one,
        jnp.swapaxes(weight_one, 1, 2) * 0.5,
        weight_two * 0.5,
        jnp.swapaxes(weight_two, 1, 2) * 0.5,
        three,
        jnp.swapaxes(three, 1, 2) * 0.5,
        dir_table.T,
    )
    core = (lax.axis_index("rep") % 2).astype(jnp.int32).reshape(1)
    gradient = shape((N_REP // 2, GRAD_ROWS, LANES), bf16)
    wide = lambda height: shape((2, height, SLOTS), bf16)
    half = lambda *outs: call(
        half_kernel,
        (wide(LAT), shape((2, 8, SLOTS)), shape((2, 8, SLOTS)), *outs),
        [pltpu.VMEM((GROUPS * LAT, LOW), bf16)],
        [smem] + [vmem] * 8,
        2000000000,
    )
    back_a, preds_a, index_a, grads_a = half(gradient)(1 - core, recv, *weights)
    from_core = lax.ppermute(grads_a, "rep", [(i, i ^ 1) for i in range(N_REP)])
    back_b, preds_b, index_b, *kept = half(wide(HID), wide(HID), wide(8), wide(HID), wide(2 * LAT), wide(HID))(
        core, recv, *weights
    )
    chip = call(
        weights_kernel,
        gradient,
        [pltpu.VMEM((N_REP // 2, GRAD_ROWS, LANES), bf16), pltpu.SemaphoreType.DMA((2,))],
        [vmem] * 7,
        0,
        hbm,
    )(*kept, from_core)
    chips = [list(range(c, N_REP, 2)) for c in range(2)]
    parts = lax.all_to_all(chip, "rep", 0, 0, tiled=True, axis_index_groups=chips)
    back = call(
        texels_kernel,
        shape((N_EXP, SEND_ROWS, LANES), bf16),
        (),
        [smem] + [vmem] * 6,
        2000000000,
    )(core, back_a, back_b, preds_a, preds_b, index_a, index_b)
    own = jnp.sum(parts.astype(f32), axis=0).astype(bf16)
    back, own = lax.optimization_barrier((back, own))
    got = lax.all_to_all(back, "exp", 0, 0, tiled=True)
    packed = lax.all_gather(own, "rep", axis=0, tiled=False)
    plane = (TEX_ROWS, LANES)
    outs = (weight_one.shape, weight_two.shape, (OUTC, 4, HID), plane, plane, plane, (OUTC, ROWS))
    grad_one, grad_two, grad_three, new_latents, new_mean, new_square, predictions = call(
        finish_kernel,
        tuple(shape(dims) for dims in outs),
        [pltpu.VMEM(dims, f32) for dims in outs] + [pltpu.SemaphoreType.DMA((10,))],
        [vmem] * 6,
        0,
        tuple([hbm] * 7),
    )(packed, got, slot, flat(latents), flat(latent_mean), flat(latent_square))
    grad_three = jnp.swapaxes(grad_three, 0, 1)
    whole = lambda a: a.reshape(latents.shape)
    return (
        whole(new_latents),
        whole(new_mean),
        whole(new_square),
        predictions,
        grad_one,
        grad_two,
        grad_three,
    )


def solution(mesh):
    in_specs = (
        P("rep", None, "exp"),
        P("rep", None, "exp"),
        P("rep", None, "exp"),
        P("exp", None, None),
        P("exp", None, None),
        P("exp", None, None),
        P(),
        P(("rep", "exp"), None),
        P(("rep", "exp")),
        P(("rep", "exp")),
        P(("rep", "exp")),
        P(None, ("rep", "exp")),
    )
    out_specs = (
        P("rep", None, "exp"),
        P("rep", None, "exp"),
        P("rep", None, "exp"),
        P(None, ("rep", "exp")),
        P("exp", None, None),
        P("exp", None, None),
        P("exp", None, None),
    )
    return jax.shard_map(on_device, mesh=mesh, in_specs=in_specs, out_specs=out_specs, check_vma=False)
```

```python
import functools

import jax
import jax.numpy as jnp
from jax import lax
from jax.experimental import pallas as pl
from jax.experimental.pallas import tpu as pltpu
from jax.sharding import PartitionSpec as P

LAT = 32
HID = 256
OUTC = 3
LANES = 128
N_EXP = 16
N_REP = 16
CAP = 64
ROWS = 2048
CHUNKS = ROWS // LANES
SLOTS = N_EXP * CAP
GROUPS = 8
LOW = 512
PIECES = 2
TEX_ROWS = 64
SEND_ROWS = TEX_ROWS + 16
GRAD_ROWS = 168

decay_one = 0.9
decay_two = 0.99
step_rate = 0.05
epsilon = 1e-08

f32 = jnp.float32
bf16 = jnp.bfloat16


def dot(a, b):
    return jnp.dot(a, b, preferred_element_type=f32)


def dot_nt(a, b):
    return lax.dot_general(a, b, (((1,), (1,)), ((), ())), preferred_element_type=f32)


def iota(shape, dim):
    return lax.broadcasted_iota(jnp.int32, shape, dim)


def hot(index, count, start=0):
    same = iota((count, index.shape[1]), 0) + start == index
    return jnp.where(same, 1.0, 0.0).astype(bf16)


def hot_wide(keys, start=0):
    column = (iota((256, LANES), 0) + start).astype(bf16)
    spread = jnp.broadcast_to(keys.astype(bf16), (256, keys.shape[1]))
    parts = [
        jnp.where(column == spread[:, i : i + LANES], jnp.ones((), bf16), jnp.zeros((), bf16))
        for i in range(0, keys.shape[1], LANES)
    ]
    return jnp.concatenate(parts, axis=1)


def split_index(rows):
    high = rows[3:4].astype(jnp.int32) - 1
    group = high >> 1
    bit = high & 1
    low = jnp.concatenate([hot_wide(jnp.where(bit == b, rows[4:5], -1.0)) for b in range(2)], axis=0)
    return group, low


def route_kernel(mat, tile_in, texel_in, direction_in, targets_in, latents_in, send, slot, *scratch):
    material_in, tile, texel, direction, targets, latents, sems = scratch
    copies = [
        pltpu.make_async_copy(source, target, sems.at[n])
        for n, (source, target) in enumerate(
            [
                (mat, material_in),
                (tile_in, tile),
                (texel_in, texel),
                (direction_in, direction),
                (targets_in, targets),
                (latents_in, latents),
            ]
        )
    ]
    for copy in copies:
        copy.start()
    for copy in copies:
        copy.wait()
    material = material_in[...]
    hots = [hot(material[i : i + 1], 64) for i in range(CHUNKS)]
    upper = jnp.where(iota((LANES, LANES), 0) <= iota((LANES, LANES), 1), 1.0, 0.0).astype(bf16)
    counted = dot(jnp.concatenate(hots, axis=0), upper)
    before = jnp.zeros((64, 1), f32)
    places = []
    for i in range(CHUNKS):
        here = counted[i * 64 : (i + 1) * 64]
        places.append(jnp.sum(hots[i].astype(f32) * (here + before), axis=0, keepdims=True))
        before = before + here[:, LANES - 1 :]
    place = jnp.concatenate(places, axis=0).astype(jnp.int32) - 1
    lane = (material & 1) * CAP + place
    pair = material >> 1
    slot[...] = pair * LANES + lane
    texels = texel[...]
    group = (texels >> 9) * 2 + tile[...]
    high = (group * 2 + ((texels >> 8) & 1) + 1).astype(f32)
    low = (texels & 255).astype(f32)
    heading = (direction[...] + 1).astype(f32)
    values = []
    lanes_hot = []
    for i in range(CHUNKS):
        row = slice(i, i + 1)
        val = jnp.concatenate(
            [
                targets[:, i * LANES : (i + 1) * LANES],
                high[row],
                low[row],
                heading[row],
                jnp.zeros((2, LANES), f32),
            ],
            axis=0,
        )
        parts = [jnp.where(pair[row] == g, val, 0.0) for g in range(32)]
        values.append(jnp.concatenate(parts, axis=0).astype(bf16))
        lanes_hot.append(hot(lane[row], LANES))
    out = dot_nt(jnp.concatenate(values, axis=1), jnp.concatenate(lanes_hot, axis=1)).astype(bf16)
    own = latents[...].astype(bf16)
    for j in range(N_EXP):
        send[j, :TEX_ROWS] = own
        send[j, TEX_ROWS:] = out[j * 16 : (j + 1) * 16]


def half_kernel(
    keep, position, recv, w_one, w_one_t, w_two, w_two_t, w_three, w_three_t, dir_t, grads, back, preds, index, tex
):
    core = position[0] & 1
    h = core if keep else 1 - core
    for b in range(4):
        for s in range(4):
            tex[b * TEX_ROWS : (b + 1) * TEX_ROWS, s * LANES : (s + 1) * LANES] = recv[4 * b + s, :TEX_ROWS]
    left = iota((8, LANES), 1) < CAP
    sides = ([], [])
    for j in range(N_EXP // 2):
        both = [recv[2 * j + s, TEX_ROWS:].astype(f32) for s in range(2)]
        first, second = [jnp.where(h == 0, v[:8], v[8:]) for v in both]
        sides[0].append(jnp.where(left, first, pltpu.roll(second, CAP, 1)))
        sides[1].append(jnp.where(left, pltpu.roll(first, CAP, 1), second))
    units = [(b, c) for b in range(2) for c in range(PIECES)]
    width = SLOTS // PIECES
    full = [jnp.concatenate(side, axis=1) for side in sides]
    for b in range(2):
        index[b] = full[b]
    rows = {(b, c): full[b][:, c * width : (c + 1) * width] for b, c in units}
    split = {n: split_index(rows[n]) for n in units}
    picked = {n: dot(tex[...], split[n][1]).reshape(GROUPS, LAT // 8, 8, width) for n in units}
    heading = {n: dot(dir_t[...], hot_wide(rows[n][5:6], 1)) for n in units}
    x = {}
    for n in units:
        wide = jnp.broadcast_to(split[n][0], (8, width))
        lat = jnp.where((wide == 0)[None], picked[n][0], 0.0)
        for r in range(1, GROUPS):
            lat = jnp.where((wide == r)[None], picked[n][r], lat)
        x[n] = jnp.concatenate([lat.reshape(LAT, width), heading[n]], axis=0).astype(bf16)
    act_one, slope_one, act_two, slope_two, misfit, delta_two, delta_one = ({} for _ in range(7))
    u = {n: dot(w_one_t[2 * h + n[0]], x[n]) for n in units}
    for n in units:
        t = jnp.tanh(u[n])
        act_one[n] = (u[n] * (1.0 + t)).astype(bf16)
        slope_one[n] = (1.0 + t) * (1.0 + u[n] * (1.0 - t))
    u = {n: dot(w_two_t[2 * h + n[0]], act_one[n]) for n in units}
    for n in units:
        t = jnp.tanh(u[n])
        act_two[n] = (u[n] * (1.0 + t)).astype(bf16)
        slope_two[n] = (1.0 + t) * (1.0 + u[n] * (1.0 - t))
    for n in units:
        b, c = n
        pred = dot(w_three[2 * h + b], act_two[n])
        preds[b, :, c * width : (c + 1) * width] = pred
        misfit[n] = jnp.where(iota((8, width), 0) < OUTC, pred - rows[n], 0.0).astype(bf16)
    half_back = {n: dot(w_three_t[2 * h + n[0]], misfit[n]) for n in units}
    for n in units:
        delta_two[n] = (half_back[n] * slope_two[n]).astype(bf16)
    half_back = {n: dot(w_two[2 * h + n[0]], delta_two[n]) for n in units}
    for b in range(2):
        pieces = [(b, c) for c in range(PIECES)]
        grad_two = sum(dot_nt(act_one[n], delta_two[n]) for n in pieces).astype(grads.dtype)
        grad_three = sum(dot_nt(misfit[n], act_two[n]) for n in pieces).astype(grads.dtype)
        for q in range(4):
            for s in range(2):
                grads[4 * b + q, s * 64 : (s + 1) * 64] = grad_two[q * 64 : (q + 1) * 64, s * LANES : (s + 1) * LANES]
            grads[4 * b + q, 160:168] = grad_three[:, (q % 2) * LANES : (q % 2 + 1) * LANES]
    for n in units:
        delta_one[n] = (half_back[n] * slope_one[n]).astype(bf16)
    for b in range(2):
        pieces = [(b, c) for c in range(PIECES)]
        grad_one = sum(dot_nt(x[n], delta_one[n]) for n in pieces).astype(grads.dtype)
        for q in range(4):
            for s in range(2):
                grads[4 * b + q, 128 + s * 16 : 128 + (s + 1) * 16] = grad_one[
                    q * 16 : (q + 1) * 16, s * LANES : (s + 1) * LANES
                ]
    for n in units:
        b, c = n
        back[b, :, c * width : (c + 1) * width] = dot(w_one[2 * h + b, :LAT], delta_one[n]).astype(bf16)


def texels_kernel(position, back_a, back_b, preds_a, preds_b, index_a, index_b, *outs):
    acc = jnp.zeros((GROUPS * LAT, LOW), f32)
    for rows_back, index in ((back_a, index_a), (back_b, index_b)):
        for b in range(2):
            rows = index[b]
            group, low_hot = split_index(rows)
            wide = jnp.broadcast_to(group.astype(bf16), (16, SLOTS))
            grad = rows_back[b].reshape(LAT // 16, 16, SLOTS)
            spread = [
                jnp.where((wide == jnp.array(r, bf16))[None], grad, jnp.zeros((), bf16)).reshape(LAT, SLOTS)
                for r in range(GROUPS)
            ]
            acc = acc + dot_nt(jnp.concatenate(spread, axis=0), low_hot)
    *outs, packets = outs
    for y in range(4):
        for x in range(4):
            packets[x, y, :TEX_ROWS] = acc[y * TEX_ROWS : (y + 1) * TEX_ROWS, x * LANES : (x + 1) * LANES].astype(bf16)
    left = iota((8, LANES), 1) < CAP
    keep = position[0] & 1
    for j in range(N_EXP // 2):
        cols = slice(j * LANES, (j + 1) * LANES)
        low, high = [], []
        for h in range(2):
            one = jnp.where(keep == h, preds_b[0, :, cols], preds_a[0, :, cols])
            two = jnp.where(keep == h, preds_b[1, :, cols], preds_a[1, :, cols])
            low.append(jnp.where(left, one, pltpu.roll(two, CAP, 1)))
            high.append(jnp.where(left, pltpu.roll(one, CAP, 1), two))
        packets[2 * j % 4, j // 2, TEX_ROWS:] = jnp.concatenate(low, axis=0).astype(bf16)
        packets[2 * j % 4 + 1, j // 2, TEX_ROWS:] = jnp.concatenate(high, axis=0).astype(bf16)
    x = position[1] & 3
    for d in range(4):
        outs[d][...] = packets[(x + d) & 3]


def relay_kernel(position, own, one, two, three, *outs):
    y = position[1] >> 2
    for d in range(4):
        to = (y + d) & 3
        parts = [part[to] for part in (own, one, two, three)]
        outs[d][:TEX_ROWS] = sum(part[:TEX_ROWS].astype(f32) for part in parts).astype(bf16)
        for n in range(4):
            outs[d][TEX_ROWS + 16 * n : TEX_ROWS + 16 * (n + 1)] = parts[n][TEX_ROWS:]


def finish_kernel(
    position, packed, got_own, got_one, got_two, got_three, slot, latents, mean, square, out_one, out_two, out_three, out_latents, out_mean, out_square, out_pred, *scratch
):
    grad_one, grad_two, grad_three, new_latents, new_mean, new_square, predictions, preds, sems = scratch
    copies = []
    gots = (got_own, got_one, got_two, got_three)

    def leave(source, target):
        copies.append(pltpu.make_async_copy(source, target, sems.at[len(copies)]))
        copies[-1].start()

    for e in range(4):
        for q in range(4):
            n = 2 * (4 * (e % 2) + q) + e // 2
            for s in range(2):
                cols = slice(s * LANES, (s + 1) * LANES)
                grad_two[e, q * 64 : (q + 1) * 64, cols] = packed[n, s * 64 : (s + 1) * 64].astype(f32)
                grad_one[e, q * 16 : (q + 1) * 16, cols] = packed[n, 128 + s * 16 : 128 + (s + 1) * 16].astype(f32)
            if q < 2:
                for c in range(OUTC):
                    grad_three[c, e : e + 1, q * LANES : (q + 1) * LANES] = packed[n, 160:168].astype(f32)[c : c + 1]
        leave(grad_two.at[e], out_two.at[e])
    leave(grad_one, out_one)
    leave(grad_three, out_three)
    texel_grad = sum(got[:TEX_ROWS].astype(f32) for got in gots)
    next_mean = decay_one * mean[...] + (1.0 - decay_one) * texel_grad
    next_square = decay_two * square[...] + (1.0 - decay_two) * texel_grad * texel_grad
    new_mean[...] = next_mean
    new_square[...] = next_square
    new_latents[...] = latents[...] - step_rate * next_mean / (jnp.sqrt(next_square) + epsilon)
    leave(new_mean, out_mean)
    leave(new_square, out_square)
    leave(new_latents, out_latents)
    y, x = position[1] >> 2, position[1] & 3
    for back_y in range(4):
        for back_x in range(4):
            first = TEX_ROWS + 16 * back_x
            preds[((y - back_y) & 3) * 4 + ((x - back_x) & 3)] = gots[back_y][first : first + 16]
    table = preds[...].reshape(N_EXP * 16, LANES)
    place = slot[...]
    lane = place & (LANES - 1)
    pair = place >> 7
    for i in range(CHUNKS):
        row = slice(i, i + 1)
        picked = dot(table, hot(lane[row], LANES))
        wide = jnp.broadcast_to(pair[row], (8, LANES))
        total = jnp.where(wide == 0, picked[:8], 0.0)
        for g in range(1, 32):
            total = jnp.where(wide == g, picked[g * 8 : (g + 1) * 8], total)
        predictions[:, i * LANES : (i + 1) * LANES] = total[:OUTC]
    leave(predictions, out_pred)
    for copy in copies:
        copy.wait()


def call(kernel, outs, scratch=(), in_specs=None, flops=0, out_specs=None):
    more = {} if in_specs is None else {"in_specs": in_specs}
    if out_specs is not None:
        more["out_specs"] = out_specs
    cost = pl.CostEstimate(flops=flops, transcendentals=0, bytes_accessed=0) if flops else None
    return pl.pallas_call(
        kernel,
        out_shape=outs,
        scratch_shapes=list(scratch),
        compiler_params=pltpu.CompilerParams(vmem_limit_bytes=32 << 20),
        cost_estimate=cost,
        **more,
    )


def shape(dims, kind=f32):
    return jax.ShapeDtypeStruct(dims, kind)


def on_device(
    latents,
    latent_mean,
    latent_square,
    weight_one,
    weight_two,
    weight_three,
    dir_table,
    materials,
    tile_ids,
    texel_ids,
    dir_ids,
    targets,
):
    flat = lambda a: a.reshape(TEX_ROWS, LANES)
    rows = lambda a: a.reshape(CHUNKS, LANES)
    hbm = pl.BlockSpec(memory_space=pltpu.HBM)
    vmem = pl.BlockSpec(memory_space=pltpu.VMEM)
    smem = pl.BlockSpec(memory_space=pltpu.SMEM)
    index_rows = pltpu.VMEM((CHUNKS, LANES), jnp.int32)
    send, slot = call(
        route_kernel,
        (shape((N_EXP, SEND_ROWS, LANES), bf16), shape((CHUNKS, LANES), jnp.int32)),
        [index_rows] * 4
        + [pltpu.VMEM((OUTC, ROWS), f32), pltpu.VMEM((TEX_ROWS, LANES), f32), pltpu.SemaphoreType.DMA((6,))],
        [hbm] * 6,
    )(*[
        pltpu.with_memory_space_constraint(a, pltpu.HBM)
        for a in (rows(materials), rows(tile_ids), rows(texel_ids), rows(dir_ids), targets, flat(latents))
    ])
    recv = lax.all_to_all(send, "exp", 0, 0, tiled=True)
    three = jnp.pad(weight_three, ((0, 0), (0, 8 - OUTC), (0, 0)))
    weights = (
        weight_one,
        jnp.swapaxes(weight_one, 1, 2) * 0.5,
        weight_two * 0.5,
        jnp.swapaxes(weight_two, 1, 2) * 0.5,
        three,
        jnp.swapaxes(three, 1, 2) * 0.5,
        dir_table.T,
    )
    position = jnp.stack([lax.axis_index("rep"), lax.axis_index("exp")]).astype(jnp.int32)
    half = lambda keep, kind: call(
        functools.partial(half_kernel, keep),
        (
            shape((N_REP // 2, GRAD_ROWS, LANES), kind),
            shape((2, LAT, SLOTS), bf16),
            shape((2, 8, SLOTS)),
            shape((2, 8, SLOTS)),
        ),
        [pltpu.VMEM((GROUPS * LAT, LOW), bf16)],
        [smem] + [vmem] * 8,
        2000000000,
    )
    grads_a, back_a, preds_a, index_a = half(False, bf16)(position, recv, *weights)
    from_core = lax.ppermute(grads_a, "rep", [(i, i ^ 1) for i in range(N_REP)])
    grads_b, back_b, preds_b, index_b = half(True, f32)(position, recv, *weights)
    chip = (grads_b + from_core.astype(f32)).astype(bf16)
    chips = [list(range(c, N_REP, 2)) for c in range(2)]
    parts = lax.all_to_all(chip, "rep", 0, 0, tiled=True, axis_index_groups=chips)
    along = lambda step_y, step_x: [
        (4 * y + x, 4 * ((y + step_y) % 4) + (x + step_x) % 4) for y in range(4) for x in range(4)
    ]
    rows_x = call(
        texels_kernel,
        tuple([shape((4, SEND_ROWS, LANES), bf16)] * 4),
        [pltpu.VMEM((4, 4, SEND_ROWS, LANES), bf16)],
        [smem] + [vmem] * 6,
        2000000000,
    )(position, back_a, back_b, preds_a, preds_b, index_a, index_b)
    got_x = [lax.ppermute(rows_x[d], "exp", along(0, d)) for d in (1, 2, 3)]
    rows_y = call(
        relay_kernel,
        tuple([shape((TEX_ROWS + 64, LANES), bf16)] * 4),
        (),
        [smem] + [vmem] * 4,
    )(position, rows_x[0], *got_x)
    got_y = [lax.ppermute(rows_y[d], "exp", along(d, 0)) for d in (1, 2, 3)]
    own = jnp.sum(parts.astype(f32), axis=0).astype(bf16)
    packed = lax.all_gather(own, "rep", axis=0, tiled=False)
    plane = (TEX_ROWS, LANES)
    outs = (weight_one.shape, weight_two.shape, (OUTC, 4, HID), plane, plane, plane, (OUTC, ROWS))
    grad_one, grad_two, grad_three, new_latents, new_mean, new_square, predictions = call(
        finish_kernel,
        tuple(shape(dims) for dims in outs),
        [pltpu.VMEM(dims, f32) for dims in outs]
        + [pltpu.VMEM((N_EXP, 16, LANES), bf16), pltpu.SemaphoreType.DMA((10,))],
        [smem] + [vmem] * 9,
        0,
        tuple([hbm] * 7),
    )(position, packed, rows_y[0], *got_y, slot, flat(latents), flat(latent_mean), flat(latent_square))
    grad_three = jnp.swapaxes(grad_three, 0, 1)
    whole = lambda a: a.reshape(latents.shape)
    return (
        whole(new_latents),
        whole(new_mean),
        whole(new_square),
        predictions,
        grad_one,
        grad_two,
        grad_three,
    )


def solution(mesh):
    in_specs = (
        P("rep", None, "exp"),
        P("rep", None, "exp"),
        P("rep", None, "exp"),
        P("exp", None, None),
        P("exp", None, None),
        P("exp", None, None),
        P(),
        P(("rep", "exp"), None),
        P(("rep", "exp")),
        P(("rep", "exp")),
        P(("rep", "exp")),
        P(None, ("rep", "exp")),
    )
    out_specs = (
        P("rep", None, "exp"),
        P("rep", None, "exp"),
        P("rep", None, "exp"),
        P(None, ("rep", "exp")),
        P("exp", None, None),
        P("exp", None, None),
        P("exp", None, None),
    )
    return jax.shard_map(on_device, mesh=mesh, in_specs=in_specs, out_specs=out_specs, check_vma=False)
```

```python
import functools

import jax
import jax.numpy as jnp
from jax import lax
from jax.experimental import pallas as pl
from jax.experimental.pallas import tpu as pltpu
from jax.sharding import PartitionSpec as P

LAT = 32
HID = 256
OUTC = 3
LANES = 128
N_EXP = 16
N_REP = 16
CAP = 64
ROWS = 2048
CHUNKS = ROWS // LANES
SLOTS = N_EXP * CAP
GROUPS = 8
LOW = 512
PIECES = 2
TEX_ROWS = 64
SEND_ROWS = TEX_ROWS + 16
GRAD_ROWS = 168

decay_one = 0.9
decay_two = 0.99
step_rate = 0.05
epsilon = 1e-08

f32 = jnp.float32
bf16 = jnp.bfloat16


def dot(a, b):
    return jnp.dot(a, b, preferred_element_type=f32)


def dot_nt(a, b):
    return lax.dot_general(a, b, (((1,), (1,)), ((), ())), preferred_element_type=f32)


def iota(shape, dim):
    return lax.broadcasted_iota(jnp.int32, shape, dim)


def hot(index, count, start=0):
    same = iota((count, index.shape[1]), 0) + start == index
    return jnp.where(same, 1.0, 0.0).astype(bf16)


def hot_wide(keys, start=0):
    column = (iota((256, LANES), 0) + start).astype(bf16)
    spread = jnp.broadcast_to(keys.astype(bf16), (256, keys.shape[1]))
    parts = [
        jnp.where(column == spread[:, i : i + LANES], jnp.ones((), bf16), jnp.zeros((), bf16))
        for i in range(0, keys.shape[1], LANES)
    ]
    return jnp.concatenate(parts, axis=1)


def split_index(rows):
    high = rows[3:4].astype(jnp.int32) - 1
    group = high >> 1
    bit = high & 1
    low = jnp.concatenate([hot_wide(jnp.where(bit == b, rows[4:5], -1.0)) for b in range(2)], axis=0)
    return group, low


def route_kernel(mat, tile_in, texel_in, direction_in, targets_in, latents_in, send, slot, *scratch):
    material_in, tile, texel, direction, targets, latents, sems = scratch
    copies = [
        pltpu.make_async_copy(source, target, sems.at[n])
        for n, (source, target) in enumerate(
            [
                (mat, material_in),
                (tile_in, tile),
                (texel_in, texel),
                (direction_in, direction),
                (targets_in, targets),
                (latents_in, latents),
            ]
        )
    ]
    for copy in copies:
        copy.start()
    for copy in copies:
        copy.wait()
    material = material_in[...]
    hots = [hot(material[i : i + 1], 64) for i in range(CHUNKS)]
    upper = jnp.where(iota((LANES, LANES), 0) <= iota((LANES, LANES), 1), 1.0, 0.0).astype(bf16)
    counted = dot(jnp.concatenate(hots, axis=0), upper)
    before = jnp.zeros((64, 1), f32)
    places = []
    for i in range(CHUNKS):
        here = counted[i * 64 : (i + 1) * 64]
        places.append(jnp.sum(hots[i].astype(f32) * (here + before), axis=0, keepdims=True))
        before = before + here[:, LANES - 1 :]
    place = jnp.concatenate(places, axis=0).astype(jnp.int32) - 1
    lane = (material & 1) * CAP + place
    pair = material >> 1
    slot[...] = pair * LANES + lane
    texels = texel[...]
    group = (texels >> 9) * 2 + tile[...]
    high = (group * 2 + ((texels >> 8) & 1) + 1).astype(f32)
    low = (texels & 255).astype(f32)
    heading = (direction[...] + 1).astype(f32)
    values = []
    lanes_hot = []
    for i in range(CHUNKS):
        row = slice(i, i + 1)
        val = jnp.concatenate(
            [
                targets[:, i * LANES : (i + 1) * LANES],
                high[row],
                low[row],
                heading[row],
                jnp.zeros((2, LANES), f32),
            ],
            axis=0,
        )
        parts = [jnp.where(pair[row] == g, val, 0.0) for g in range(32)]
        values.append(jnp.concatenate(parts, axis=0).astype(bf16))
        lanes_hot.append(hot(lane[row], LANES))
    out = dot_nt(jnp.concatenate(values, axis=1), jnp.concatenate(lanes_hot, axis=1)).astype(bf16)
    own = latents[...].astype(bf16)
    for j in range(N_EXP):
        send[j, :TEX_ROWS] = own
        send[j, TEX_ROWS:] = out[j * 16 : (j + 1) * 16]


def half_kernel(
    keep, core_at, recv, w_one, w_one_t, w_two, w_two_t, w_three, w_three_t, dir_t, grads, back, preds, index, tex
):
    core = core_at[0]
    h = core if keep else 1 - core
    for b in range(4):
        for s in range(4):
            tex[b * TEX_ROWS : (b + 1) * TEX_ROWS, s * LANES : (s + 1) * LANES] = recv[4 * b + s, :TEX_ROWS]
    left = iota((8, LANES), 1) < CAP
    sides = ([], [])
    for j in range(N_EXP // 2):
        both = [recv[2 * j + s, TEX_ROWS:].astype(f32) for s in range(2)]
        first, second = [jnp.where(h == 0, v[:8], v[8:]) for v in both]
        sides[0].append(jnp.where(left, first, pltpu.roll(second, CAP, 1)))
        sides[1].append(jnp.where(left, pltpu.roll(first, CAP, 1), second))
    units = [(b, c) for b in range(2) for c in range(PIECES)]
    width = SLOTS // PIECES
    full = [jnp.concatenate(side, axis=1) for side in sides]
    for b in range(2):
        index[b] = full[b]
    rows = {(b, c): full[b][:, c * width : (c + 1) * width] for b, c in units}
    split = {n: split_index(rows[n]) for n in units}
    picked = {n: dot(tex[...], split[n][1]).reshape(GROUPS, LAT // 8, 8, width) for n in units}
    heading = {n: dot(dir_t[...], hot_wide(rows[n][5:6], 1)) for n in units}
    x = {}
    for n in units:
        wide = jnp.broadcast_to(split[n][0], (8, width))
        lat = jnp.where((wide == 0)[None], picked[n][0], 0.0)
        for r in range(1, GROUPS):
            lat = jnp.where((wide == r)[None], picked[n][r], lat)
        x[n] = jnp.concatenate([lat.reshape(LAT, width), heading[n]], axis=0).astype(bf16)
    act_one, slope_one, act_two, slope_two, misfit, delta_two, delta_one = ({} for _ in range(7))
    u = {n: dot(w_one_t[2 * h + n[0]], x[n]) for n in units}
    for n in units:
        t = jnp.tanh(u[n])
        act_one[n] = (u[n] * (1.0 + t)).astype(bf16)
        slope_one[n] = (1.0 + t) * (1.0 + u[n] * (1.0 - t))
    u = {n: dot(w_two_t[2 * h + n[0]], act_one[n]) for n in units}
    for n in units:
        t = jnp.tanh(u[n])
        act_two[n] = (u[n] * (1.0 + t)).astype(bf16)
        slope_two[n] = (1.0 + t) * (1.0 + u[n] * (1.0 - t))
    for n in units:
        b, c = n
        pred = dot(w_three[2 * h + b], act_two[n])
        preds[b, :, c * width : (c + 1) * width] = pred
        misfit[n] = jnp.where(iota((8, width), 0) < OUTC, pred - rows[n], 0.0).astype(bf16)
    half_back = {n: dot(w_three_t[2 * h + n[0]], misfit[n]) for n in units}
    for n in units:
        delta_two[n] = (half_back[n] * slope_two[n]).astype(bf16)
    half_back = {n: dot(w_two[2 * h + n[0]], delta_two[n]) for n in units}
    for b in range(2):
        pieces = [(b, c) for c in range(PIECES)]
        grad_two = sum(dot_nt(act_one[n], delta_two[n]) for n in pieces).astype(grads.dtype)
        grad_three = sum(dot_nt(misfit[n], act_two[n]) for n in pieces).astype(grads.dtype)
        for q in range(4):
            for s in range(2):
                grads[4 * b + q, s * 64 : (s + 1) * 64] = grad_two[q * 64 : (q + 1) * 64, s * LANES : (s + 1) * LANES]
            grads[4 * b + q, 160:168] = grad_three[:, (q % 2) * LANES : (q % 2 + 1) * LANES]
    for n in units:
        delta_one[n] = (half_back[n] * slope_one[n]).astype(bf16)
    for b in range(2):
        pieces = [(b, c) for c in range(PIECES)]
        grad_one = sum(dot_nt(x[n], delta_one[n]) for n in pieces).astype(grads.dtype)
        for q in range(4):
            for s in range(2):
                grads[4 * b + q, 128 + s * 16 : 128 + (s + 1) * 16] = grad_one[
                    q * 16 : (q + 1) * 16, s * LANES : (s + 1) * LANES
                ]
    for n in units:
        b, c = n
        back[b, :, c * width : (c + 1) * width] = dot(w_one[2 * h + b, :LAT], delta_one[n]).astype(bf16)


def texels_kernel(core_at, x_at, back_a, back_b, preds_a, preds_b, index_a, index_b, *outs):
    acc = jnp.zeros((GROUPS * LAT, LOW), f32)
    for rows_back, index in ((back_a, index_a), (back_b, index_b)):
        for b in range(2):
            rows = index[b]
            group, low_hot = split_index(rows)
            wide = jnp.broadcast_to(group.astype(bf16), (16, SLOTS))
            grad = rows_back[b].reshape(LAT // 16, 16, SLOTS)
            spread = [
                jnp.where((wide == jnp.array(r, bf16))[None], grad, jnp.zeros((), bf16)).reshape(LAT, SLOTS)
                for r in range(GROUPS)
            ]
            acc = acc + dot_nt(jnp.concatenate(spread, axis=0), low_hot)
    *outs, packets = outs
    for y in range(4):
        for x in range(4):
            packets[x, y, :TEX_ROWS] = acc[y * TEX_ROWS : (y + 1) * TEX_ROWS, x * LANES : (x + 1) * LANES].astype(bf16)
    left = iota((8, LANES), 1) < CAP
    keep = core_at[0]
    for j in range(N_EXP // 2):
        cols = slice(j * LANES, (j + 1) * LANES)
        low, high = [], []
        for h in range(2):
            one = jnp.where(keep == h, preds_b[0, :, cols], preds_a[0, :, cols])
            two = jnp.where(keep == h, preds_b[1, :, cols], preds_a[1, :, cols])
            low.append(jnp.where(left, one, pltpu.roll(two, CAP, 1)))
            high.append(jnp.where(left, pltpu.roll(one, CAP, 1), two))
        packets[2 * j % 4, j // 2, TEX_ROWS:] = jnp.concatenate(low, axis=0).astype(bf16)
        packets[2 * j % 4 + 1, j // 2, TEX_ROWS:] = jnp.concatenate(high, axis=0).astype(bf16)
    x = x_at[0]
    for d in range(4):
        outs[d][...] = packets[(x + d) & 3]


def relay_kernel(y_at, own, one, two, three, *outs):
    y = y_at[0]
    for d in range(4):
        to = (y + d) & 3
        parts = [part[to] for part in (own, one, two, three)]
        outs[d][:TEX_ROWS] = sum(part[:TEX_ROWS].astype(f32) for part in parts).astype(bf16)
        for n in range(4):
            outs[d][TEX_ROWS + 16 * n : TEX_ROWS + 16 * (n + 1)] = parts[n][TEX_ROWS:]


def finish_kernel(
    y_at, x_at, packed, got_own, got_one, got_two, got_three, slot, latents, mean, square, out_one, out_two, out_three, out_latents, out_mean, out_square, out_pred, *scratch
):
    grad_one, grad_two, grad_three, new_latents, new_mean, new_square, predictions, preds, sems = scratch
    copies = []
    gots = (got_own, got_one, got_two, got_three)

    def leave(source, target):
        copies.append(pltpu.make_async_copy(source, target, sems.at[len(copies)]))
        copies[-1].start()

    for e in range(4):
        for q in range(4):
            n = 2 * (4 * (e % 2) + q) + e // 2
            for s in range(2):
                cols = slice(s * LANES, (s + 1) * LANES)
                grad_two[e, q * 64 : (q + 1) * 64, cols] = packed[n, s * 64 : (s + 1) * 64].astype(f32)
                grad_one[e, q * 16 : (q + 1) * 16, cols] = packed[n, 128 + s * 16 : 128 + (s + 1) * 16].astype(f32)
            if q < 2:
                for c in range(OUTC):
                    grad_three[c, e : e + 1, q * LANES : (q + 1) * LANES] = packed[n, 160:168].astype(f32)[c : c + 1]
        leave(grad_two.at[e], out_two.at[e])
    leave(grad_one, out_one)
    leave(grad_three, out_three)
    texel_grad = sum(got[:TEX_ROWS].astype(f32) for got in gots)
    next_mean = decay_one * mean[...] + (1.0 - decay_one) * texel_grad
    next_square = decay_two * square[...] + (1.0 - decay_two) * texel_grad * texel_grad
    new_mean[...] = next_mean
    new_square[...] = next_square
    new_latents[...] = latents[...] - step_rate * next_mean / (jnp.sqrt(next_square) + epsilon)
    leave(new_mean, out_mean)
    leave(new_square, out_square)
    leave(new_latents, out_latents)
    y, x = y_at[0], x_at[0]
    for back_y in range(4):
        for back_x in range(4):
            first = TEX_ROWS + 16 * back_x
            preds[((y - back_y) & 3) * 4 + ((x - back_x) & 3)] = gots[back_y][first : first + 16]
    table = preds[...].reshape(N_EXP * 16, LANES)
    place = slot[...]
    lane = place & (LANES - 1)
    pair = place >> 7
    for i in range(CHUNKS):
        row = slice(i, i + 1)
        picked = dot(table, hot(lane[row], LANES))
        wide = jnp.broadcast_to(pair[row], (8, LANES))
        total = jnp.where(wide == 0, picked[:8], 0.0)
        for g in range(1, 32):
            total = jnp.where(wide == g, picked[g * 8 : (g + 1) * 8], total)
        predictions[:, i * LANES : (i + 1) * LANES] = total[:OUTC]
    leave(predictions, out_pred)
    for copy in copies:
        copy.wait()


def call(kernel, outs, scratch=(), in_specs=None, flops=0, out_specs=None):
    more = {} if in_specs is None else {"in_specs": in_specs}
    if out_specs is not None:
        more["out_specs"] = out_specs
    cost = pl.CostEstimate(flops=flops, transcendentals=0, bytes_accessed=0) if flops else None
    return pl.pallas_call(
        kernel,
        out_shape=outs,
        scratch_shapes=list(scratch),
        compiler_params=pltpu.CompilerParams(vmem_limit_bytes=32 << 20),
        cost_estimate=cost,
        **more,
    )


def shape(dims, kind=f32):
    return jax.ShapeDtypeStruct(dims, kind)


def on_device(
    latents,
    latent_mean,
    latent_square,
    weight_one,
    weight_two,
    weight_three,
    dir_table,
    materials,
    tile_ids,
    texel_ids,
    dir_ids,
    targets,
):
    flat = lambda a: a.reshape(TEX_ROWS, LANES)
    rows = lambda a: a.reshape(CHUNKS, LANES)
    hbm = pl.BlockSpec(memory_space=pltpu.HBM)
    vmem = pl.BlockSpec(memory_space=pltpu.VMEM)
    smem = pl.BlockSpec(memory_space=pltpu.SMEM)
    index_rows = pltpu.VMEM((CHUNKS, LANES), jnp.int32)
    send, slot = call(
        route_kernel,
        (shape((N_EXP, SEND_ROWS, LANES), bf16), shape((CHUNKS, LANES), jnp.int32)),
        [index_rows] * 4
        + [pltpu.VMEM((OUTC, ROWS), f32), pltpu.VMEM((TEX_ROWS, LANES), f32), pltpu.SemaphoreType.DMA((6,))],
        [hbm] * 6,
    )(*[
        pltpu.with_memory_space_constraint(a, pltpu.HBM)
        for a in (rows(materials), rows(tile_ids), rows(texel_ids), rows(dir_ids), targets, flat(latents))
    ])
    recv = lax.all_to_all(send, "exp", 0, 0, tiled=True)
    three = jnp.pad(weight_three, ((0, 0), (0, 8 - OUTC), (0, 0)))
    weights = (
        weight_one,
        jnp.swapaxes(weight_one, 1, 2) * 0.5,
        weight_two * 0.5,
        jnp.swapaxes(weight_two, 1, 2) * 0.5,
        three,
        jnp.swapaxes(three, 1, 2) * 0.5,
        dir_table.T,
    )
    core = (lax.axis_index("rep") & 1).astype(jnp.int32).reshape(1)
    at_y = (lax.axis_index("exp") >> 2).astype(jnp.int32).reshape(1)
    at_x = (lax.axis_index("exp") & 3).astype(jnp.int32).reshape(1)
    half = lambda keep, kind: call(
        functools.partial(half_kernel, keep),
        (
            shape((N_REP // 2, GRAD_ROWS, LANES), kind),
            shape((2, LAT, SLOTS), bf16),
            shape((2, 8, SLOTS)),
            shape((2, 8, SLOTS)),
        ),
        [pltpu.VMEM((GROUPS * LAT, LOW), bf16)],
        [smem] + [vmem] * 8,
        2000000000,
    )
    grads_a, back_a, preds_a, index_a = half(False, bf16)(core, recv, *weights)
    from_core = lax.ppermute(grads_a, "rep", [(i, i ^ 1) for i in range(N_REP)])
    grads_b, back_b, preds_b, index_b = half(True, f32)(core, recv, *weights)
    chip = (grads_b + from_core.astype(f32)).astype(bf16)
    chips = [list(range(c, N_REP, 2)) for c in range(2)]
    parts = lax.all_to_all(chip, "rep", 0, 0, tiled=True, axis_index_groups=chips)
    along = lambda step_y, step_x: [
        (4 * y + x, 4 * ((y + step_y) % 4) + (x + step_x) % 4) for y in range(4) for x in range(4)
    ]
    rows_x = call(
        texels_kernel,
        tuple([shape((4, SEND_ROWS, LANES), bf16)] * 4),
        [pltpu.VMEM((4, 4, SEND_ROWS, LANES), bf16)],
        [smem] * 2 + [vmem] * 6,
        2000000000,
    )(core, at_x, back_a, back_b, preds_a, preds_b, index_a, index_b)
    got_x = {d: lax.ppermute(rows_x[d], "exp", along(0, d)) for d in (2, 1, 3)}
    rows_y = call(
        relay_kernel,
        tuple([shape((TEX_ROWS + 64, LANES), bf16)] * 4),
        (),
        [smem] + [vmem] * 4,
    )(at_y, rows_x[0], got_x[1], got_x[2], got_x[3])
    got_y = {d: lax.ppermute(rows_y[d], "exp", along(d, 0)) for d in (2, 1, 3)}
    own = jnp.sum(parts.astype(f32), axis=0).astype(bf16)
    packed = lax.all_gather(own, "rep", axis=0, tiled=False)
    plane = (TEX_ROWS, LANES)
    outs = (weight_one.shape, weight_two.shape, (OUTC, 4, HID), plane, plane, plane, (OUTC, ROWS))
    grad_one, grad_two, grad_three, new_latents, new_mean, new_square, predictions = call(
        finish_kernel,
        tuple(shape(dims) for dims in outs),
        [pltpu.VMEM(dims, f32) for dims in outs]
        + [pltpu.VMEM((N_EXP, 16, LANES), bf16), pltpu.SemaphoreType.DMA((10,))],
        [smem] * 2 + [vmem] * 9,
        0,
        tuple([hbm] * 7),
    )(at_y, at_x, packed, rows_y[0], got_y[1], got_y[2], got_y[3], slot, flat(latents), flat(latent_mean), flat(latent_square))
    grad_three = jnp.swapaxes(grad_three, 0, 1)
    whole = lambda a: a.reshape(latents.shape)
    return (
        whole(new_latents),
        whole(new_mean),
        whole(new_square),
        predictions,
        grad_one,
        grad_two,
        grad_three,
    )


def solution(mesh):
    in_specs = (
        P("rep", None, "exp"),
        P("rep", None, "exp"),
        P("rep", None, "exp"),
        P("exp", None, None),
        P("exp", None, None),
        P("exp", None, None),
        P(),
        P(("rep", "exp"), None),
        P(("rep", "exp")),
        P(("rep", "exp")),
        P(("rep", "exp")),
        P(None, ("rep", "exp")),
    )
    out_specs = (
        P("rep", None, "exp"),
        P("rep", None, "exp"),
        P("rep", None, "exp"),
        P(None, ("rep", "exp")),
        P("exp", None, None),
        P("exp", None, None),
        P("exp", None, None),
    )
    return jax.shard_map(on_device, mesh=mesh, in_specs=in_specs, out_specs=out_specs, check_vma=False)
```

```python
import functools

import jax
import jax.numpy as jnp
from jax import lax
from jax.experimental import pallas as pl
from jax.experimental.pallas import tpu as pltpu
from jax.sharding import PartitionSpec as P

LAT = 32
HID = 256
OUTC = 3
LANES = 128
N_EXP = 16
N_REP = 16
CAP = 64
ROWS = 2048
CHUNKS = ROWS // LANES
SLOTS = N_EXP * CAP
GROUPS = 8
LOW = 512
PIECES = 2
TEX_ROWS = 64
SEND_ROWS = TEX_ROWS + 16
GRAD_ROWS = 168
BACK_ROWS = TEX_ROWS + 8
RELAY_ROWS = TEX_ROWS + 4 * 8

decay_one = 0.9
decay_two = 0.99
step_rate = 0.05
epsilon = 1e-08

f32 = jnp.float32
bf16 = jnp.bfloat16


def dot(a, b):
    return jnp.dot(a, b, preferred_element_type=f32)


def dot_nt(a, b):
    return lax.dot_general(a, b, (((1,), (1,)), ((), ())), preferred_element_type=f32)


def iota(shape, dim):
    return lax.broadcasted_iota(jnp.int32, shape, dim)


def hot(index, count, start=0):
    same = iota((count, index.shape[1]), 0) + start == index
    return jnp.where(same, 1.0, 0.0).astype(bf16)


def hot_wide(keys, start=0):
    column = (iota((256, LANES), 0) + start).astype(bf16)
    spread = jnp.broadcast_to(keys.astype(bf16), (256, keys.shape[1]))
    parts = [
        jnp.where(column == spread[:, i : i + LANES], jnp.ones((), bf16), jnp.zeros((), bf16))
        for i in range(0, keys.shape[1], LANES)
    ]
    return jnp.concatenate(parts, axis=1)


def split_index(rows):
    high = rows[3:4].astype(jnp.int32) - 1
    group = high >> 1
    bit = high & 1
    low = jnp.concatenate([hot_wide(jnp.where(bit == b, rows[4:5], -1.0)) for b in range(2)], axis=0)
    return group, low


def route_kernel(mat, tile_in, texel_in, direction_in, targets_in, latents_in, send, slot, *scratch):
    material_in, tile, texel, direction, targets, latents, sems = scratch
    copies = [
        pltpu.make_async_copy(source, target, sems.at[n])
        for n, (source, target) in enumerate(
            [
                (mat, material_in),
                (tile_in, tile),
                (texel_in, texel),
                (direction_in, direction),
                (targets_in, targets),
                (latents_in, latents),
            ]
        )
    ]
    for copy in copies:
        copy.start()
    for copy in copies:
        copy.wait()
    material = material_in[...]
    hots = [hot(material[i : i + 1], 64) for i in range(CHUNKS)]
    upper = jnp.where(iota((LANES, LANES), 0) <= iota((LANES, LANES), 1), 1.0, 0.0).astype(bf16)
    counted = dot(jnp.concatenate(hots, axis=0), upper)
    before = jnp.zeros((64, 1), f32)
    places = []
    for i in range(CHUNKS):
        here = counted[i * 64 : (i + 1) * 64]
        places.append(jnp.sum(hots[i].astype(f32) * (here + before), axis=0, keepdims=True))
        before = before + here[:, LANES - 1 :]
    place = jnp.concatenate(places, axis=0).astype(jnp.int32) - 1
    lane = (material & 1) * CAP + place
    pair = material >> 1
    slot[...] = pair * LANES + lane
    texels = texel[...]
    group = (texels >> 9) * 2 + tile[...]
    high = (group * 2 + ((texels >> 8) & 1) + 1).astype(f32)
    low = (texels & 255).astype(f32)
    heading = (direction[...] + 1).astype(f32)
    values = []
    lanes_hot = []
    for i in range(CHUNKS):
        row = slice(i, i + 1)
        val = jnp.concatenate(
            [
                targets[:, i * LANES : (i + 1) * LANES],
                high[row],
                low[row],
                heading[row],
                jnp.zeros((2, LANES), f32),
            ],
            axis=0,
        )
        parts = [jnp.where(pair[row] == g, val, 0.0) for g in range(32)]
        values.append(jnp.concatenate(parts, axis=0).astype(bf16))
        lanes_hot.append(hot(lane[row], LANES))
    out = dot_nt(jnp.concatenate(values, axis=1), jnp.concatenate(lanes_hot, axis=1)).astype(bf16)
    own = latents[...].astype(bf16)
    for j in range(N_EXP):
        send[j, :TEX_ROWS] = own
        send[j, TEX_ROWS:] = out[j * 16 : (j + 1) * 16]


def half_kernel(
    keep, core_at, recv, w_one, w_one_t, w_two, w_two_t, w_three, w_three_t, dir_t, grads, back, preds, index, tex
):
    core = core_at[0]
    h = core if keep else 1 - core
    for b in range(4):
        for s in range(4):
            tex[b * TEX_ROWS : (b + 1) * TEX_ROWS, s * LANES : (s + 1) * LANES] = recv[4 * b + s, :TEX_ROWS]
    left = iota((8, LANES), 1) < CAP
    sides = ([], [])
    for j in range(N_EXP // 2):
        both = [recv[2 * j + s, TEX_ROWS:].astype(f32) for s in range(2)]
        first, second = [jnp.where(h == 0, v[:8], v[8:]) for v in both]
        sides[0].append(jnp.where(left, first, pltpu.roll(second, CAP, 1)))
        sides[1].append(jnp.where(left, pltpu.roll(first, CAP, 1), second))
    units = [(b, c) for b in range(2) for c in range(PIECES)]
    width = SLOTS // PIECES
    full = [jnp.concatenate(side, axis=1) for side in sides]
    for b in range(2):
        index[b] = full[b]
    rows = {(b, c): full[b][:, c * width : (c + 1) * width] for b, c in units}
    split = {n: split_index(rows[n]) for n in units}
    picked = {n: dot(tex[...], split[n][1]).reshape(GROUPS, LAT // 8, 8, width) for n in units}
    heading = {n: dot(dir_t[...], hot_wide(rows[n][5:6], 1)) for n in units}
    x = {}
    for n in units:
        wide = jnp.broadcast_to(split[n][0], (8, width))
        lat = jnp.where((wide == 0)[None], picked[n][0], 0.0)
        for r in range(1, GROUPS):
            lat = jnp.where((wide == r)[None], picked[n][r], lat)
        x[n] = jnp.concatenate([lat.reshape(LAT, width), heading[n]], axis=0).astype(bf16)
    act_one, slope_one, act_two, slope_two, misfit, delta_two, delta_one = ({} for _ in range(7))
    u = {n: dot(w_one_t[2 * h + n[0]], x[n]) for n in units}
    for n in units:
        t = jnp.tanh(u[n])
        act_one[n] = (u[n] * (1.0 + t)).astype(bf16)
        slope_one[n] = (1.0 + t) * (1.0 + u[n] * (1.0 - t))
    u = {n: dot(w_two_t[2 * h + n[0]], act_one[n]) for n in units}
    for n in units:
        t = jnp.tanh(u[n])
        act_two[n] = (u[n] * (1.0 + t)).astype(bf16)
        slope_two[n] = (1.0 + t) * (1.0 + u[n] * (1.0 - t))
    for n in units:
        b, c = n
        pred = dot(w_three[2 * h + b], act_two[n])
        preds[b, :, c * width : (c + 1) * width] = pred
        misfit[n] = jnp.where(iota((8, width), 0) < OUTC, pred - rows[n], 0.0).astype(bf16)
    half_back = {n: dot(w_three_t[2 * h + n[0]], misfit[n]) for n in units}
    for n in units:
        delta_two[n] = (half_back[n] * slope_two[n]).astype(bf16)
    half_back = {n: dot(w_two[2 * h + n[0]], delta_two[n]) for n in units}
    for b in range(2):
        pieces = [(b, c) for c in range(PIECES)]
        grad_two = sum(dot_nt(act_one[n], delta_two[n]) for n in pieces).astype(grads.dtype)
        grad_three = sum(dot_nt(misfit[n], act_two[n]) for n in pieces).astype(grads.dtype)
        for q in range(4):
            for s in range(2):
                grads[4 * b + q, s * 64 : (s + 1) * 64] = grad_two[q * 64 : (q + 1) * 64, s * LANES : (s + 1) * LANES]
            grads[4 * b + q, 160:168] = grad_three[:, (q % 2) * LANES : (q % 2 + 1) * LANES]
    for n in units:
        delta_one[n] = (half_back[n] * slope_one[n]).astype(bf16)
    for b in range(2):
        pieces = [(b, c) for c in range(PIECES)]
        grad_one = sum(dot_nt(x[n], delta_one[n]) for n in pieces).astype(grads.dtype)
        for q in range(4):
            for s in range(2):
                grads[4 * b + q, 128 + s * 16 : 128 + (s + 1) * 16] = grad_one[
                    q * 16 : (q + 1) * 16, s * LANES : (s + 1) * LANES
                ]
    for n in units:
        b, c = n
        back[b, :, c * width : (c + 1) * width] = dot(w_one[2 * h + b, :LAT], delta_one[n]).astype(bf16)


def texels_kernel(core_at, x_at, back_a, back_b, preds_a, preds_b, index_a, index_b, *outs):
    acc = jnp.zeros((GROUPS * LAT, LOW), f32)
    for rows_back, index in ((back_a, index_a), (back_b, index_b)):
        for b in range(2):
            rows = index[b]
            group, low_hot = split_index(rows)
            wide = jnp.broadcast_to(group.astype(bf16), (16, SLOTS))
            grad = rows_back[b].reshape(LAT // 16, 16, SLOTS)
            spread = [
                jnp.where((wide == jnp.array(r, bf16))[None], grad, jnp.zeros((), bf16)).reshape(LAT, SLOTS)
                for r in range(GROUPS)
            ]
            acc = acc + dot_nt(jnp.concatenate(spread, axis=0), low_hot)
    *outs, packets = outs
    for y in range(4):
        for x in range(4):
            packets[x, y, :TEX_ROWS] = acc[y * TEX_ROWS : (y + 1) * TEX_ROWS, x * LANES : (x + 1) * LANES].astype(bf16)
    left = iota((8, LANES), 1) < CAP
    keep = core_at[0]
    for j in range(N_EXP // 2):
        cols = slice(j * LANES, (j + 1) * LANES)
        low, high = [], []
        for h in range(2):
            one = jnp.where(keep == h, preds_b[0, :, cols], preds_a[0, :, cols])
            two = jnp.where(keep == h, preds_b[1, :, cols], preds_a[1, :, cols])
            low.append(jnp.where(left, one, pltpu.roll(two, CAP, 1)))
            high.append(jnp.where(left, pltpu.roll(one, CAP, 1), two))
        packets[2 * j % 4, j // 2, TEX_ROWS:] = (low[0] + pltpu.roll(low[1], 4, 0)).astype(bf16)
        packets[2 * j % 4 + 1, j // 2, TEX_ROWS:] = (high[0] + pltpu.roll(high[1], 4, 0)).astype(bf16)
    x = x_at[0]
    for d in range(4):
        outs[d][...] = packets[(x + d) & 3]


def relay_kernel(y_at, own, one, two, three, *outs):
    y = y_at[0]
    for d in range(4):
        to = (y + d) & 3
        parts = [part[to] for part in (own, one, two, three)]
        outs[d][:TEX_ROWS] = sum(part[:TEX_ROWS].astype(f32) for part in parts).astype(bf16)
        for n in range(4):
            outs[d][TEX_ROWS + 8 * n : TEX_ROWS + 8 * (n + 1)] = parts[n][TEX_ROWS:]


def finish_kernel(
    y_at, x_at, packed, got_own, got_one, got_two, got_three, slot, latents, mean, square, out_one, out_two, out_three, out_latents, out_mean, out_square, out_pred, *scratch
):
    grad_one, grad_two, grad_three, new_latents, new_mean, new_square, predictions, preds, sems = scratch
    copies = []
    gots = (got_own, got_one, got_two, got_three)

    def leave(source, target):
        copies.append(pltpu.make_async_copy(source, target, sems.at[len(copies)]))
        copies[-1].start()

    for e in range(4):
        for q in range(4):
            n = 2 * (4 * (e % 2) + q) + e // 2
            for s in range(2):
                cols = slice(s * LANES, (s + 1) * LANES)
                grad_two[e, q * 64 : (q + 1) * 64, cols] = packed[n, s * 64 : (s + 1) * 64].astype(f32)
                grad_one[e, q * 16 : (q + 1) * 16, cols] = packed[n, 128 + s * 16 : 128 + (s + 1) * 16].astype(f32)
            if q < 2:
                for c in range(OUTC):
                    grad_three[c, e : e + 1, q * LANES : (q + 1) * LANES] = packed[n, 160:168].astype(f32)[c : c + 1]
        leave(grad_two.at[e], out_two.at[e])
    leave(grad_one, out_one)
    leave(grad_three, out_three)
    texel_grad = sum(got[:TEX_ROWS].astype(f32) for got in gots)
    next_mean = decay_one * mean[...] + (1.0 - decay_one) * texel_grad
    next_square = decay_two * square[...] + (1.0 - decay_two) * texel_grad * texel_grad
    new_mean[...] = next_mean
    new_square[...] = next_square
    new_latents[...] = latents[...] - step_rate * next_mean / (jnp.sqrt(next_square) + epsilon)
    leave(new_mean, out_mean)
    leave(new_square, out_square)
    leave(new_latents, out_latents)
    y, x = y_at[0], x_at[0]
    for back_y in range(4):
        for back_x in range(4):
            first = TEX_ROWS + 8 * back_x
            preds[((y - back_y) & 3) * 4 + ((x - back_x) & 3)] = gots[back_y][first : first + 8].astype(f32)
    table = preds[...].reshape(N_EXP * 8, LANES).astype(bf16)
    place = slot[...]
    lane = place & (LANES - 1)
    pair = place >> 7
    for i in range(CHUNKS):
        row = slice(i, i + 1)
        picked = dot(table, hot(lane[row], LANES))
        owner = jnp.broadcast_to(pair[row] >> 1, (8, LANES))
        total = jnp.where(owner == 0, picked[:8], 0.0)
        for j in range(1, N_EXP):
            total = jnp.where(owner == j, picked[j * 8 : (j + 1) * 8], total)
        predictions[:, i * LANES : (i + 1) * LANES] = jnp.where((pair[row] & 1) == 0, total, pltpu.roll(total, 4, 0))[:OUTC]
    leave(predictions, out_pred)
    for copy in copies:
        copy.wait()


def call(kernel, outs, scratch=(), in_specs=None, flops=0, out_specs=None):
    more = {} if in_specs is None else {"in_specs": in_specs}
    if out_specs is not None:
        more["out_specs"] = out_specs
    cost = pl.CostEstimate(flops=flops, transcendentals=0, bytes_accessed=0) if flops else None
    return pl.pallas_call(
        kernel,
        out_shape=outs,
        scratch_shapes=list(scratch),
        compiler_params=pltpu.CompilerParams(vmem_limit_bytes=32 << 20),
        cost_estimate=cost,
        **more,
    )


def shape(dims, kind=f32):
    return jax.ShapeDtypeStruct(dims, kind)


def on_device(
    latents,
    latent_mean,
    latent_square,
    weight_one,
    weight_two,
    weight_three,
    dir_table,
    materials,
    tile_ids,
    texel_ids,
    dir_ids,
    targets,
):
    flat = lambda a: a.reshape(TEX_ROWS, LANES)
    rows = lambda a: a.reshape(CHUNKS, LANES)
    hbm = pl.BlockSpec(memory_space=pltpu.HBM)
    vmem = pl.BlockSpec(memory_space=pltpu.VMEM)
    smem = pl.BlockSpec(memory_space=pltpu.SMEM)
    index_rows = pltpu.VMEM((CHUNKS, LANES), jnp.int32)
    send, slot = call(
        route_kernel,
        (shape((N_EXP, SEND_ROWS, LANES), bf16), shape((CHUNKS, LANES), jnp.int32)),
        [index_rows] * 4
        + [pltpu.VMEM((OUTC, ROWS), f32), pltpu.VMEM((TEX_ROWS, LANES), f32), pltpu.SemaphoreType.DMA((6,))],
        [hbm] * 6,
    )(*[
        pltpu.with_memory_space_constraint(a, pltpu.HBM)
        for a in (rows(materials), rows(tile_ids), rows(texel_ids), rows(dir_ids), targets, flat(latents))
    ])
    recv = lax.all_to_all(send, "exp", 0, 0, tiled=True)
    three = jnp.pad(weight_three, ((0, 0), (0, 8 - OUTC), (0, 0)))
    weights = (
        weight_one,
        jnp.swapaxes(weight_one, 1, 2) * 0.5,
        weight_two * 0.5,
        jnp.swapaxes(weight_two, 1, 2) * 0.5,
        three,
        jnp.swapaxes(three, 1, 2) * 0.5,
        dir_table.T,
    )
    core = (lax.axis_index("rep") & 1).astype(jnp.int32).reshape(1)
    at_y = (lax.axis_index("exp") >> 2).astype(jnp.int32).reshape(1)
    at_x = (lax.axis_index("exp") & 3).astype(jnp.int32).reshape(1)
    half = lambda keep, kind: call(
        functools.partial(half_kernel, keep),
        (
            shape((N_REP // 2, GRAD_ROWS, LANES), kind),
            shape((2, LAT, SLOTS), bf16),
            shape((2, 8, SLOTS)),
            shape((2, 8, SLOTS)),
        ),
        [pltpu.VMEM((GROUPS * LAT, LOW), bf16)],
        [smem] + [vmem] * 8,
        2000000000,
    )
    grads_a, back_a, preds_a, index_a = half(False, bf16)(core, recv, *weights)
    from_core = lax.ppermute(grads_a, "rep", [(i, i ^ 1) for i in range(N_REP)])
    grads_b, back_b, preds_b, index_b = half(True, f32)(core, recv, *weights)
    chip = (grads_b + from_core.astype(f32)).astype(bf16)
    chips = [list(range(c, N_REP, 2)) for c in range(2)]
    parts = lax.all_to_all(chip, "rep", 0, 0, tiled=True, axis_index_groups=chips)
    along = lambda step_y, step_x: [
        (4 * y + x, 4 * ((y + step_y) % 4) + (x + step_x) % 4) for y in range(4) for x in range(4)
    ]
    rows_x = call(
        texels_kernel,
        tuple([shape((4, BACK_ROWS, LANES), bf16)] * 4),
        [pltpu.VMEM((4, 4, BACK_ROWS, LANES), bf16)],
        [smem] * 2 + [vmem] * 6,
        2000000000,
    )(core, at_x, back_a, back_b, preds_a, preds_b, index_a, index_b)
    got_x = {d: lax.ppermute(rows_x[d], "exp", along(0, d)) for d in (2, 1, 3)}
    rows_y = call(
        relay_kernel,
        tuple([shape((RELAY_ROWS, LANES), bf16)] * 4),
        (),
        [smem] + [vmem] * 4,
    )(at_y, rows_x[0], got_x[1], got_x[2], got_x[3])
    got_y = {d: lax.ppermute(rows_y[d], "exp", along(d, 0)) for d in (2, 1, 3)}
    own = jnp.sum(parts.astype(f32), axis=0).astype(bf16)
    packed = lax.all_gather(own, "rep", axis=0, tiled=False)
    plane = (TEX_ROWS, LANES)
    outs = (weight_one.shape, weight_two.shape, (OUTC, 4, HID), plane, plane, plane, (OUTC, ROWS))
    grad_one, grad_two, grad_three, new_latents, new_mean, new_square, predictions = call(
        finish_kernel,
        tuple(shape(dims) for dims in outs),
        [pltpu.VMEM(dims, f32) for dims in outs]
        + [pltpu.VMEM((N_EXP, 8, LANES), f32), pltpu.SemaphoreType.DMA((10,))],
        [smem] * 2 + [vmem] * 9,
        0,
        tuple([hbm] * 7),
    )(at_y, at_x, packed, rows_y[0], got_y[1], got_y[2], got_y[3], slot, flat(latents), flat(latent_mean), flat(latent_square))
    grad_three = jnp.swapaxes(grad_three, 0, 1)
    whole = lambda a: a.reshape(latents.shape)
    return (
        whole(new_latents),
        whole(new_mean),
        whole(new_square),
        predictions,
        grad_one,
        grad_two,
        grad_three,
    )


def solution(mesh):
    in_specs = (
        P("rep", None, "exp"),
        P("rep", None, "exp"),
        P("rep", None, "exp"),
        P("exp", None, None),
        P("exp", None, None),
        P("exp", None, None),
        P(),
        P(("rep", "exp"), None),
        P(("rep", "exp")),
        P(("rep", "exp")),
        P(("rep", "exp")),
        P(None, ("rep", "exp")),
    )
    out_specs = (
        P("rep", None, "exp"),
        P("rep", None, "exp"),
        P("rep", None, "exp"),
        P(None, ("rep", "exp")),
        P("exp", None, None),
        P("exp", None, None),
        P("exp", None, None),
    )
    return jax.shard_map(on_device, mesh=mesh, in_specs=in_specs, out_specs=out_specs, check_vma=False)
```

```python
import functools

import jax
import jax.numpy as jnp
from jax import lax
from jax.experimental import pallas as pl
from jax.experimental.pallas import tpu as pltpu
from jax.sharding import PartitionSpec as P

LAT = 32
HID = 256
OUTC = 3
LANES = 128
N_EXP = 16
N_REP = 16
CAP = 64
ROWS = 2048
CHUNKS = ROWS // LANES
SLOTS = N_EXP * CAP
GROUPS = 8
LOW = 512
PIECES = 2
TEX_ROWS = 64
SEND_ROWS = TEX_ROWS + 16
GRAD_ROWS = 168
BACK_ROWS = TEX_ROWS + 8
RELAY_ROWS = TEX_ROWS + 4 * 8

decay_one = 0.9
decay_two = 0.99
step_rate = 0.05
epsilon = 1e-08

f32 = jnp.float32
bf16 = jnp.bfloat16


def dot(a, b):
    return jnp.dot(a, b, preferred_element_type=f32)


def dot_nt(a, b):
    return lax.dot_general(a, b, (((1,), (1,)), ((), ())), preferred_element_type=f32)


def iota(shape, dim):
    return lax.broadcasted_iota(jnp.int32, shape, dim)


def hot(index, count, start=0):
    same = iota((count, index.shape[1]), 0) + start == index
    return jnp.where(same, 1.0, 0.0).astype(bf16)


def hot_wide(keys, start=0):
    column = (iota((256, LANES), 0) + start).astype(bf16)
    spread = jnp.broadcast_to(keys.astype(bf16), (256, keys.shape[1]))
    parts = [
        jnp.where(column == spread[:, i : i + LANES], jnp.ones((), bf16), jnp.zeros((), bf16))
        for i in range(0, keys.shape[1], LANES)
    ]
    return jnp.concatenate(parts, axis=1)


def split_index(rows):
    high = rows[3:4].astype(jnp.int32) - 1
    group = high >> 1
    bit = high & 1
    low = jnp.concatenate([hot_wide(jnp.where(bit == b, rows[4:5], -1.0)) for b in range(2)], axis=0)
    return group, low


def route_kernel(mat, tile_in, texel_in, direction_in, targets_in, latents_in, send, slot, *scratch):
    material_in, tile, texel, direction, targets, latents, sems = scratch
    copies = [
        pltpu.make_async_copy(source, target, sems.at[n])
        for n, (source, target) in enumerate(
            [
                (mat, material_in),
                (tile_in, tile),
                (texel_in, texel),
                (direction_in, direction),
                (targets_in, targets),
                (latents_in, latents),
            ]
        )
    ]
    for copy in copies:
        copy.start()
    for copy in copies:
        copy.wait()
    material = material_in[...]
    hots = [hot(material[i : i + 1], 64) for i in range(CHUNKS)]
    upper = jnp.where(iota((LANES, LANES), 0) <= iota((LANES, LANES), 1), 1.0, 0.0).astype(bf16)
    counted = dot(jnp.concatenate(hots, axis=0), upper)
    before = jnp.zeros((64, 1), f32)
    places = []
    for i in range(CHUNKS):
        here = counted[i * 64 : (i + 1) * 64]
        places.append(jnp.sum(hots[i].astype(f32) * (here + before), axis=0, keepdims=True))
        before = before + here[:, LANES - 1 :]
    place = jnp.concatenate(places, axis=0).astype(jnp.int32) - 1
    lane = (material & 1) * CAP + place
    pair = material >> 1
    slot[...] = pair * LANES + lane
    texels = texel[...]
    group = (texels >> 9) * 2 + tile[...]
    high = (group * 2 + ((texels >> 8) & 1) + 1).astype(f32)
    low = (texels & 255).astype(f32)
    heading = (direction[...] + 1).astype(f32)
    values = []
    lanes_hot = []
    for i in range(CHUNKS):
        row = slice(i, i + 1)
        val = jnp.concatenate(
            [
                targets[:, i * LANES : (i + 1) * LANES],
                high[row],
                low[row],
                heading[row],
                jnp.zeros((2, LANES), f32),
            ],
            axis=0,
        )
        parts = [jnp.where(pair[row] == g, val, 0.0) for g in range(32)]
        values.append(jnp.concatenate(parts, axis=0).astype(bf16))
        lanes_hot.append(hot(lane[row], LANES))
    out = dot_nt(jnp.concatenate(values, axis=1), jnp.concatenate(lanes_hot, axis=1)).astype(bf16)
    own = latents[...].astype(bf16)
    for j in range(N_EXP):
        send[j, :TEX_ROWS] = own
        send[j, TEX_ROWS:] = out[j * 16 : (j + 1) * 16]


def half_kernel(
    keep, core_at, recv, w_one, w_one_t, w_two, w_two_t, w_three, w_three_t, dir_t, grads, back, preds, index, tex
):
    core = core_at[0]
    h = core if keep else 1 - core
    for b in range(4):
        for s in range(4):
            tex[b * TEX_ROWS : (b + 1) * TEX_ROWS, s * LANES : (s + 1) * LANES] = recv[4 * b + s, :TEX_ROWS]
    left = iota((8, LANES), 1) < CAP
    sides = ([], [])
    for j in range(N_EXP // 2):
        both = [recv[2 * j + s, TEX_ROWS:].astype(f32) for s in range(2)]
        first, second = [jnp.where(h == 0, v[:8], v[8:]) for v in both]
        sides[0].append(jnp.where(left, first, pltpu.roll(second, CAP, 1)))
        sides[1].append(jnp.where(left, pltpu.roll(first, CAP, 1), second))
    units = [(b, c) for b in range(2) for c in range(PIECES)]
    width = SLOTS // PIECES
    full = [jnp.concatenate(side, axis=1) for side in sides]
    for b in range(2):
        index[b] = full[b]
    rows = {(b, c): full[b][:, c * width : (c + 1) * width] for b, c in units}
    split = {n: split_index(rows[n]) for n in units}
    picked = {n: dot(tex[...], split[n][1]).reshape(GROUPS, LAT // 8, 8, width) for n in units}
    heading = {n: dot(dir_t[...], hot_wide(rows[n][5:6], 1)) for n in units}
    x = {}
    for n in units:
        wide = jnp.broadcast_to(split[n][0], (8, width))
        lat = jnp.where((wide == 0)[None], picked[n][0], 0.0)
        for r in range(1, GROUPS):
            lat = jnp.where((wide == r)[None], picked[n][r], lat)
        x[n] = jnp.concatenate([lat.reshape(LAT, width), heading[n]], axis=0).astype(bf16)
    act_one, slope_one, act_two, slope_two, misfit, delta_two, delta_one = ({} for _ in range(7))
    u = {n: dot(w_one_t[2 * h + n[0]], x[n]) for n in units}
    for n in units:
        t = jnp.tanh(u[n])
        act_one[n] = (u[n] * (1.0 + t)).astype(bf16)
        slope_one[n] = (1.0 + t) * (1.0 + u[n] * (1.0 - t))
    u = {n: dot(w_two_t[2 * h + n[0]], act_one[n]) for n in units}
    for n in units:
        t = jnp.tanh(u[n])
        act_two[n] = (u[n] * (1.0 + t)).astype(bf16)
        slope_two[n] = (1.0 + t) * (1.0 + u[n] * (1.0 - t))
    for n in units:
        b, c = n
        pred = dot(w_three[2 * h + b], act_two[n])
        preds[b, :, c * width : (c + 1) * width] = pred
        misfit[n] = jnp.where(iota((8, width), 0) < OUTC, pred - rows[n], 0.0).astype(bf16)
    half_back = {n: dot(w_three_t[2 * h + n[0]], misfit[n]) for n in units}
    for n in units:
        delta_two[n] = (half_back[n] * slope_two[n]).astype(bf16)
    half_back = {n: dot(w_two[2 * h + n[0]], delta_two[n]) for n in units}
    for b in range(2):
        pieces = [(b, c) for c in range(PIECES)]
        grad_two = sum(dot_nt(act_one[n], delta_two[n]) for n in pieces).astype(grads.dtype)
        grad_three = sum(dot_nt(misfit[n], act_two[n]) for n in pieces).astype(grads.dtype)
        for q in range(4):
            for s in range(2):
                grads[4 * b + q, s * 64 : (s + 1) * 64] = grad_two[q * 64 : (q + 1) * 64, s * LANES : (s + 1) * LANES]
            grads[4 * b + q, 160:168] = grad_three[:, (q % 2) * LANES : (q % 2 + 1) * LANES]
    for n in units:
        delta_one[n] = (half_back[n] * slope_one[n]).astype(bf16)
    for b in range(2):
        pieces = [(b, c) for c in range(PIECES)]
        grad_one = sum(dot_nt(x[n], delta_one[n]) for n in pieces).astype(grads.dtype)
        for q in range(4):
            for s in range(2):
                grads[4 * b + q, 128 + s * 16 : 128 + (s + 1) * 16] = grad_one[
                    q * 16 : (q + 1) * 16, s * LANES : (s + 1) * LANES
                ]
    for n in units:
        b, c = n
        back[b, :, c * width : (c + 1) * width] = dot(w_one[2 * h + b, :LAT], delta_one[n]).astype(bf16)


def texels_kernel(core_at, x_at, back_a, back_b, preds_a, preds_b, index_a, index_b, *outs):
    acc = jnp.zeros((GROUPS * LAT, LOW), f32)
    for rows_back, index in ((back_a, index_a), (back_b, index_b)):
        for b in range(2):
            rows = index[b]
            group, low_hot = split_index(rows)
            wide = jnp.broadcast_to(group.astype(bf16), (16, SLOTS))
            grad = rows_back[b].reshape(LAT // 16, 16, SLOTS)
            spread = [
                jnp.where((wide == jnp.array(r, bf16))[None], grad, jnp.zeros((), bf16)).reshape(LAT, SLOTS)
                for r in range(GROUPS)
            ]
            acc = acc + dot_nt(jnp.concatenate(spread, axis=0), low_hot)
    *outs, packets = outs
    for y in range(4):
        for x in range(4):
            packets[x, y, :TEX_ROWS] = acc[y * TEX_ROWS : (y + 1) * TEX_ROWS, x * LANES : (x + 1) * LANES].astype(bf16)
    left = iota((8, LANES), 1) < CAP
    keep = core_at[0]
    for j in range(N_EXP // 2):
        cols = slice(j * LANES, (j + 1) * LANES)
        low, high = [], []
        for h in range(2):
            one = jnp.where(keep == h, preds_b[0, :, cols], preds_a[0, :, cols])
            two = jnp.where(keep == h, preds_b[1, :, cols], preds_a[1, :, cols])
            low.append(jnp.where(left, one, pltpu.roll(two, CAP, 1)))
            high.append(jnp.where(left, pltpu.roll(one, CAP, 1), two))
        packets[2 * j % 4, j // 2, TEX_ROWS:] = (low[0] + pltpu.roll(low[1], 4, 0)).astype(bf16)
        packets[2 * j % 4 + 1, j // 2, TEX_ROWS:] = (high[0] + pltpu.roll(high[1], 4, 0)).astype(bf16)
    x = x_at[0]
    for d in range(4):
        outs[d][...] = packets[(x + d) & 3]


def relay_kernel(y_at, own, two, one, three, *outs):
    y = y_at[0]
    for d in range(4):
        to = (y + d) & 3
        parts = [part[to] for part in (own, one, two, three)]
        outs[d][:TEX_ROWS] = sum(part[:TEX_ROWS].astype(f32) for part in parts).astype(bf16)
        for n in range(4):
            outs[d][TEX_ROWS + 8 * n : TEX_ROWS + 8 * (n + 1)] = parts[n][TEX_ROWS:]


def finish_kernel(
    y_at, x_at, packed, got_own, got_two, got_one, got_three, slot, latents, mean, square, out_one, out_two, out_three, out_latents, out_mean, out_square, out_pred, *scratch
):
    grad_one, grad_two, grad_three, new_latents, new_mean, new_square, predictions, preds, sems = scratch
    copies = []
    gots = (got_own, got_one, got_two, got_three)

    def leave(source, target):
        copies.append(pltpu.make_async_copy(source, target, sems.at[len(copies)]))
        copies[-1].start()

    for e in range(4):
        for q in range(4):
            n = 2 * (4 * (e % 2) + q) + e // 2
            for s in range(2):
                cols = slice(s * LANES, (s + 1) * LANES)
                grad_two[e, q * 64 : (q + 1) * 64, cols] = packed[n, s * 64 : (s + 1) * 64].astype(f32)
                grad_one[e, q * 16 : (q + 1) * 16, cols] = packed[n, 128 + s * 16 : 128 + (s + 1) * 16].astype(f32)
            if q < 2:
                for c in range(OUTC):
                    grad_three[c, e : e + 1, q * LANES : (q + 1) * LANES] = packed[n, 160:168].astype(f32)[c : c + 1]
        leave(grad_two.at[e], out_two.at[e])
    leave(grad_one, out_one)
    leave(grad_three, out_three)
    texel_grad = sum(got[:TEX_ROWS].astype(f32) for got in gots)
    next_mean = decay_one * mean[...] + (1.0 - decay_one) * texel_grad
    next_square = decay_two * square[...] + (1.0 - decay_two) * texel_grad * texel_grad
    new_mean[...] = next_mean
    new_square[...] = next_square
    new_latents[...] = latents[...] - step_rate * next_mean / (jnp.sqrt(next_square) + epsilon)
    leave(new_mean, out_mean)
    leave(new_square, out_square)
    leave(new_latents, out_latents)
    y, x = y_at[0], x_at[0]
    for back_y in range(4):
        for back_x in range(4):
            first = TEX_ROWS + 8 * back_x
            preds[((y - back_y) & 3) * 4 + ((x - back_x) & 3)] = gots[back_y][first : first + 8].astype(f32)
    table = preds[...].reshape(N_EXP * 8, LANES).astype(bf16)
    place = slot[...]
    lane = place & (LANES - 1)
    pair = place >> 7
    for i in range(CHUNKS):
        row = slice(i, i + 1)
        picked = dot(table, hot(lane[row], LANES))
        owner = jnp.broadcast_to(pair[row] >> 1, (8, LANES))
        total = jnp.where(owner == 0, picked[:8], 0.0)
        for j in range(1, N_EXP):
            total = jnp.where(owner == j, picked[j * 8 : (j + 1) * 8], total)
        predictions[:, i * LANES : (i + 1) * LANES] = jnp.where((pair[row] & 1) == 0, total, pltpu.roll(total, 4, 0))[:OUTC]
    leave(predictions, out_pred)
    for copy in copies:
        copy.wait()


def call(kernel, outs, scratch=(), in_specs=None, flops=0, out_specs=None):
    more = {} if in_specs is None else {"in_specs": in_specs}
    if out_specs is not None:
        more["out_specs"] = out_specs
    cost = pl.CostEstimate(flops=flops, transcendentals=0, bytes_accessed=0) if flops else None
    return pl.pallas_call(
        kernel,
        out_shape=outs,
        scratch_shapes=list(scratch),
        compiler_params=pltpu.CompilerParams(vmem_limit_bytes=32 << 20),
        cost_estimate=cost,
        **more,
    )


def shape(dims, kind=f32):
    return jax.ShapeDtypeStruct(dims, kind)


def on_device(
    latents,
    latent_mean,
    latent_square,
    weight_one,
    weight_two,
    weight_three,
    dir_table,
    materials,
    tile_ids,
    texel_ids,
    dir_ids,
    targets,
):
    flat = lambda a: a.reshape(TEX_ROWS, LANES)
    rows = lambda a: a.reshape(CHUNKS, LANES)
    hbm = pl.BlockSpec(memory_space=pltpu.HBM)
    vmem = pl.BlockSpec(memory_space=pltpu.VMEM)
    smem = pl.BlockSpec(memory_space=pltpu.SMEM)
    index_rows = pltpu.VMEM((CHUNKS, LANES), jnp.int32)
    send, slot = call(
        route_kernel,
        (shape((N_EXP, SEND_ROWS, LANES), bf16), shape((CHUNKS, LANES), jnp.int32)),
        [index_rows] * 4
        + [pltpu.VMEM((OUTC, ROWS), f32), pltpu.VMEM((TEX_ROWS, LANES), f32), pltpu.SemaphoreType.DMA((6,))],
        [hbm] * 6,
    )(*[
        pltpu.with_memory_space_constraint(a, pltpu.HBM)
        for a in (rows(materials), rows(tile_ids), rows(texel_ids), rows(dir_ids), targets, flat(latents))
    ])
    recv = lax.all_to_all(send, "exp", 0, 0, tiled=True)
    three = jnp.pad(weight_three, ((0, 0), (0, 8 - OUTC), (0, 0)))
    weights = (
        weight_one,
        jnp.swapaxes(weight_one, 1, 2) * 0.5,
        weight_two * 0.5,
        jnp.swapaxes(weight_two, 1, 2) * 0.5,
        three,
        jnp.swapaxes(three, 1, 2) * 0.5,
        dir_table.T,
    )
    core = (lax.axis_index("rep") & 1).astype(jnp.int32).reshape(1)
    at_y = (lax.axis_index("exp") >> 2).astype(jnp.int32).reshape(1)
    at_x = (lax.axis_index("exp") & 3).astype(jnp.int32).reshape(1)
    half = lambda keep, kind: call(
        functools.partial(half_kernel, keep),
        (
            shape((N_REP // 2, GRAD_ROWS, LANES), kind),
            shape((2, LAT, SLOTS), bf16),
            shape((2, 8, SLOTS)),
            shape((2, 8, SLOTS)),
        ),
        [pltpu.VMEM((GROUPS * LAT, LOW), bf16)],
        [smem] + [vmem] * 8,
        2000000000,
    )
    grads_a, back_a, preds_a, index_a = half(False, bf16)(core, recv, *weights)
    from_core = lax.ppermute(grads_a, "rep", [(i, i ^ 1) for i in range(N_REP)])
    grads_b, back_b, preds_b, index_b = half(True, f32)(core, recv, *weights)
    chip = (grads_b + from_core.astype(f32)).astype(bf16)
    chips = [list(range(c, N_REP, 2)) for c in range(2)]
    parts = lax.all_to_all(chip, "rep", 0, 0, tiled=True, axis_index_groups=chips)
    along = lambda step_y, step_x: [
        (4 * y + x, 4 * ((y + step_y) % 4) + (x + step_x) % 4) for y in range(4) for x in range(4)
    ]
    rows_x = call(
        texels_kernel,
        tuple([shape((4, BACK_ROWS, LANES), bf16)] * 4),
        [pltpu.VMEM((4, 4, BACK_ROWS, LANES), bf16)],
        [smem] * 2 + [vmem] * 6,
        2000000000,
    )(core, at_x, back_a, back_b, preds_a, preds_b, index_a, index_b)
    got_x = {d: lax.ppermute(rows_x[d], "exp", along(0, d)) for d in (2, 1, 3)}
    rows_y = call(
        relay_kernel,
        tuple([shape((RELAY_ROWS, LANES), bf16)] * 4),
        (),
        [smem] + [vmem] * 4,
    )(at_y, rows_x[0], got_x[2], got_x[1], got_x[3])
    got_y = {d: lax.ppermute(rows_y[d], "exp", along(d, 0)) for d in (2, 1, 3)}
    own = jnp.sum(parts.astype(f32), axis=0).astype(bf16)
    packed = lax.all_gather(own, "rep", axis=0, tiled=False)
    plane = (TEX_ROWS, LANES)
    outs = (weight_one.shape, weight_two.shape, (OUTC, 4, HID), plane, plane, plane, (OUTC, ROWS))
    grad_one, grad_two, grad_three, new_latents, new_mean, new_square, predictions = call(
        finish_kernel,
        tuple(shape(dims) for dims in outs),
        [pltpu.VMEM(dims, f32) for dims in outs]
        + [pltpu.VMEM((N_EXP, 8, LANES), f32), pltpu.SemaphoreType.DMA((10,))],
        [smem] * 2 + [vmem] * 9,
        0,
        tuple([hbm] * 7),
    )(at_y, at_x, packed, rows_y[0], got_y[2], got_y[1], got_y[3], slot, flat(latents), flat(latent_mean), flat(latent_square))
    grad_three = jnp.swapaxes(grad_three, 0, 1)
    whole = lambda a: a.reshape(latents.shape)
    return (
        whole(new_latents),
        whole(new_mean),
        whole(new_square),
        predictions,
        grad_one,
        grad_two,
        grad_three,
    )


def solution(mesh):
    in_specs = (
        P("rep", None, "exp"),
        P("rep", None, "exp"),
        P("rep", None, "exp"),
        P("exp", None, None),
        P("exp", None, None),
        P("exp", None, None),
        P(),
        P(("rep", "exp"), None),
        P(("rep", "exp")),
        P(("rep", "exp")),
        P(("rep", "exp")),
        P(None, ("rep", "exp")),
    )
    out_specs = (
        P("rep", None, "exp"),
        P("rep", None, "exp"),
        P("rep", None, "exp"),
        P(None, ("rep", "exp")),
        P("exp", None, None),
        P("exp", None, None),
        P("exp", None, None),
    )
    return jax.shard_map(on_device, mesh=mesh, in_specs=in_specs, out_specs=out_specs, check_vma=False)
```

```python
import functools

import jax
import jax.numpy as jnp
from jax import lax
from jax.experimental import pallas as pl
from jax.experimental.pallas import tpu as pltpu
from jax.sharding import PartitionSpec as P

LAT = 32
HID = 256
OUTC = 3
LANES = 128
N_EXP = 16
N_REP = 16
CAP = 64
ROWS = 2048
CHUNKS = ROWS // LANES
SLOTS = N_EXP * CAP
GROUPS = 16
LOW = 256
PIECES = 2
TEX_ROWS = 64
SEND_ROWS = TEX_ROWS + 16
GRAD_ROWS = 168
BACK_ROWS = TEX_ROWS + 8
RELAY_ROWS = TEX_ROWS + 4 * 8

decay_one = 0.9
decay_two = 0.99
step_rate = 0.05
epsilon = 1e-08

f32 = jnp.float32
bf16 = jnp.bfloat16


def dot(a, b):
    return jnp.dot(a, b, preferred_element_type=f32)


def dot_nt(a, b):
    return lax.dot_general(a, b, (((1,), (1,)), ((), ())), preferred_element_type=f32)


def iota(shape, dim):
    return lax.broadcasted_iota(jnp.int32, shape, dim)


def hot(index, count, start=0):
    same = iota((count, index.shape[1]), 0) + start == index
    return jnp.where(same, 1.0, 0.0).astype(bf16)


def hot_wide(keys, start=0):
    column = (iota((256, LANES), 0) + start).astype(bf16)
    spread = jnp.broadcast_to(keys.astype(bf16), (256, keys.shape[1]))
    parts = [
        jnp.where(column == spread[:, i : i + LANES], jnp.ones((), bf16), jnp.zeros((), bf16))
        for i in range(0, keys.shape[1], LANES)
    ]
    return jnp.concatenate(parts, axis=1)


def split_index(rows):
    return rows[3:4] - 1.0, hot_wide(rows[4:5])


def route_kernel(mat, tile_in, texel_in, direction_in, targets_in, latents_in, send, slot, *scratch):
    material_in, tile, texel, direction, targets, latents, sems = scratch
    copies = [
        pltpu.make_async_copy(source, target, sems.at[n])
        for n, (source, target) in enumerate(
            [
                (mat, material_in),
                (tile_in, tile),
                (texel_in, texel),
                (direction_in, direction),
                (targets_in, targets),
                (latents_in, latents),
            ]
        )
    ]
    for copy in copies:
        copy.start()
    for copy in copies:
        copy.wait()
    material = material_in[...]
    hots = [hot(material[i : i + 1], 64) for i in range(CHUNKS)]
    upper = jnp.where(iota((LANES, LANES), 0) <= iota((LANES, LANES), 1), 1.0, 0.0).astype(bf16)
    counted = dot(jnp.concatenate(hots, axis=0), upper)
    before = jnp.zeros((64, 1), f32)
    places = []
    for i in range(CHUNKS):
        here = counted[i * 64 : (i + 1) * 64]
        places.append(jnp.sum(hots[i].astype(f32) * (here + before), axis=0, keepdims=True))
        before = before + here[:, LANES - 1 :]
    place = jnp.concatenate(places, axis=0).astype(jnp.int32) - 1
    lane = (material & 1) * CAP + place
    pair = material >> 1
    slot[...] = pair * LANES + lane
    texels = texel[...]
    high = ((texels >> 8) * 2 + tile[...] + 1).astype(f32)
    low = (texels & 255).astype(f32)
    heading = (direction[...] + 1).astype(f32)
    values = []
    lanes_hot = []
    for i in range(CHUNKS):
        row = slice(i, i + 1)
        val = jnp.concatenate(
            [
                targets[:, i * LANES : (i + 1) * LANES],
                high[row],
                low[row],
                heading[row],
                jnp.zeros((2, LANES), f32),
            ],
            axis=0,
        )
        parts = [jnp.where(pair[row] == g, val, 0.0) for g in range(32)]
        values.append(jnp.concatenate(parts, axis=0).astype(bf16))
        lanes_hot.append(hot(lane[row], LANES))
    out = dot_nt(jnp.concatenate(values, axis=1), jnp.concatenate(lanes_hot, axis=1)).astype(bf16)
    own = latents[...].astype(bf16)
    for j in range(N_EXP):
        send[j, :TEX_ROWS] = own
        send[j, TEX_ROWS:] = out[j * 16 : (j + 1) * 16]


def half_kernel(
    keep, core_at, recv, w_one, w_one_t, w_two, w_two_t, w_three, w_three_t, dir_t, grads, back, preds, index, tex
):
    core = core_at[0]
    h = core if keep else 1 - core
    for b in range(8):
        for s in range(2):
            tex[b * TEX_ROWS : (b + 1) * TEX_ROWS, s * LANES : (s + 1) * LANES] = recv[2 * b + s, :TEX_ROWS]
    left = iota((8, LANES), 1) < CAP
    sides = ([], [])
    for j in range(N_EXP // 2):
        both = [recv[2 * j + s, TEX_ROWS:].astype(f32) for s in range(2)]
        first, second = [jnp.where(h == 0, v[:8], v[8:]) for v in both]
        sides[0].append(jnp.where(left, first, pltpu.roll(second, CAP, 1)))
        sides[1].append(jnp.where(left, pltpu.roll(first, CAP, 1), second))
    units = [(b, c) for b in range(2) for c in range(PIECES)]
    width = SLOTS // PIECES
    full = [jnp.concatenate(side, axis=1) for side in sides]
    for b in range(2):
        index[b] = full[b]
    rows = {(b, c): full[b][:, c * width : (c + 1) * width] for b, c in units}
    split = {n: split_index(rows[n]) for n in units}
    picked = {n: dot(tex[...], split[n][1]).reshape(GROUPS, LAT // 8, 8, width) for n in units}
    heading = {n: dot(dir_t[...], hot_wide(rows[n][5:6], 1)) for n in units}
    x = {}
    for n in units:
        wide = jnp.broadcast_to(split[n][0], (8, width))
        lat = jnp.where((wide == 0)[None], picked[n][0], 0.0)
        for r in range(1, GROUPS):
            lat = jnp.where((wide == r)[None], picked[n][r], lat)
        x[n] = jnp.concatenate([lat.reshape(LAT, width), heading[n]], axis=0).astype(bf16)
    act_one, slope_one, act_two, slope_two, misfit, delta_two, delta_one = ({} for _ in range(7))
    u = {n: dot(w_one_t[2 * h + n[0]], x[n]) for n in units}
    for n in units:
        t = jnp.tanh(u[n])
        act_one[n] = (u[n] * (1.0 + t)).astype(bf16)
        slope_one[n] = (1.0 + t) * (1.0 + u[n] * (1.0 - t))
    u = {n: dot(w_two_t[2 * h + n[0]], act_one[n]) for n in units}
    for n in units:
        t = jnp.tanh(u[n])
        act_two[n] = (u[n] * (1.0 + t)).astype(bf16)
        slope_two[n] = (1.0 + t) * (1.0 + u[n] * (1.0 - t))
    for n in units:
        b, c = n
        pred = dot(w_three[2 * h + b], act_two[n])
        preds[b, :, c * width : (c + 1) * width] = pred
        misfit[n] = jnp.where(iota((8, width), 0) < OUTC, pred - rows[n], 0.0).astype(bf16)
    half_back = {n: dot(w_three_t[2 * h + n[0]], misfit[n]) for n in units}
    for n in units:
        delta_two[n] = (half_back[n] * slope_two[n]).astype(bf16)
    half_back = {n: dot(w_two[2 * h + n[0]], delta_two[n]) for n in units}
    for b in range(2):
        pieces = [(b, c) for c in range(PIECES)]
        grad_two = sum(dot_nt(act_one[n], delta_two[n]) for n in pieces).astype(grads.dtype)
        grad_three = sum(dot_nt(misfit[n], act_two[n]) for n in pieces).astype(grads.dtype)
        for q in range(4):
            for s in range(2):
                grads[4 * b + q, s * 64 : (s + 1) * 64] = grad_two[q * 64 : (q + 1) * 64, s * LANES : (s + 1) * LANES]
            grads[4 * b + q, 160:168] = grad_three[:, (q % 2) * LANES : (q % 2 + 1) * LANES]
    for n in units:
        delta_one[n] = (half_back[n] * slope_one[n]).astype(bf16)
    for b in range(2):
        pieces = [(b, c) for c in range(PIECES)]
        grad_one = sum(dot_nt(x[n], delta_one[n]) for n in pieces).astype(grads.dtype)
        for q in range(4):
            for s in range(2):
                grads[4 * b + q, 128 + s * 16 : 128 + (s + 1) * 16] = grad_one[
                    q * 16 : (q + 1) * 16, s * LANES : (s + 1) * LANES
                ]
    for n in units:
        b, c = n
        back[b, :, c * width : (c + 1) * width] = dot(w_one[2 * h + b, :LAT], delta_one[n]).astype(bf16)


def texels_kernel(core_at, x_at, back_a, back_b, preds_a, preds_b, index_a, index_b, *outs):
    acc = jnp.zeros((GROUPS * LAT, LOW), f32)
    for rows_back, index in ((back_a, index_a), (back_b, index_b)):
        for b in range(2):
            rows = index[b]
            group, low_hot = split_index(rows)
            wide = jnp.broadcast_to(group.astype(bf16), (16, SLOTS))
            grad = rows_back[b].reshape(LAT // 16, 16, SLOTS)
            spread = [
                jnp.where((wide == jnp.array(r, bf16))[None], grad, jnp.zeros((), bf16)).reshape(LAT, SLOTS)
                for r in range(GROUPS)
            ]
            acc = acc + dot_nt(jnp.concatenate(spread, axis=0), low_hot)
    *outs, packets = outs
    for y in range(4):
        for x in range(4):
            first = (2 * y + x // 2) * TEX_ROWS
            packets[x, y, :TEX_ROWS] = acc[first : first + TEX_ROWS, x % 2 * LANES : (x % 2 + 1) * LANES].astype(bf16)
    left = iota((8, LANES), 1) < CAP
    keep = core_at[0]
    for j in range(N_EXP // 2):
        cols = slice(j * LANES, (j + 1) * LANES)
        low, high = [], []
        for h in range(2):
            one = jnp.where(keep == h, preds_b[0, :, cols], preds_a[0, :, cols])
            two = jnp.where(keep == h, preds_b[1, :, cols], preds_a[1, :, cols])
            low.append(jnp.where(left, one, pltpu.roll(two, CAP, 1)))
            high.append(jnp.where(left, pltpu.roll(one, CAP, 1), two))
        packets[2 * j % 4, j // 2, TEX_ROWS:] = (low[0] + pltpu.roll(low[1], 4, 0)).astype(bf16)
        packets[2 * j % 4 + 1, j // 2, TEX_ROWS:] = (high[0] + pltpu.roll(high[1], 4, 0)).astype(bf16)
    x = x_at[0]
    for d in range(4):
        outs[d][...] = packets[(x + d) & 3]


def relay_kernel(y_at, own, two, one, three, *outs):
    y = y_at[0]
    for d in range(4):
        to = (y + d) & 3
        parts = [part[to] for part in (own, one, two, three)]
        outs[d][:TEX_ROWS] = sum(part[:TEX_ROWS].astype(f32) for part in parts).astype(bf16)
        for n in range(4):
            outs[d][TEX_ROWS + 8 * n : TEX_ROWS + 8 * (n + 1)] = parts[n][TEX_ROWS:]


def finish_kernel(
    y_at, x_at, packed, got_own, got_two, got_one, got_three, slot, latents, mean, square, out_one, out_two, out_three, out_latents, out_mean, out_square, out_pred, *scratch
):
    grad_one, grad_two, grad_three, new_latents, new_mean, new_square, predictions, preds, sems = scratch
    copies = []
    gots = (got_own, got_one, got_two, got_three)

    def leave(source, target):
        copies.append(pltpu.make_async_copy(source, target, sems.at[len(copies)]))
        copies[-1].start()

    for e in range(4):
        for q in range(4):
            n = 2 * (4 * (e % 2) + q) + e // 2
            for s in range(2):
                cols = slice(s * LANES, (s + 1) * LANES)
                grad_two[e, q * 64 : (q + 1) * 64, cols] = packed[n, s * 64 : (s + 1) * 64].astype(f32)
                grad_one[e, q * 16 : (q + 1) * 16, cols] = packed[n, 128 + s * 16 : 128 + (s + 1) * 16].astype(f32)
            if q < 2:
                for c in range(OUTC):
                    grad_three[c, e : e + 1, q * LANES : (q + 1) * LANES] = packed[n, 160:168].astype(f32)[c : c + 1]
        leave(grad_two.at[e], out_two.at[e])
    leave(grad_one, out_one)
    leave(grad_three, out_three)
    texel_grad = sum(got[:TEX_ROWS].astype(f32) for got in gots)
    next_mean = decay_one * mean[...] + (1.0 - decay_one) * texel_grad
    next_square = decay_two * square[...] + (1.0 - decay_two) * texel_grad * texel_grad
    new_mean[...] = next_mean
    new_square[...] = next_square
    new_latents[...] = latents[...] - step_rate * next_mean / (jnp.sqrt(next_square) + epsilon)
    leave(new_mean, out_mean)
    leave(new_square, out_square)
    leave(new_latents, out_latents)
    y, x = y_at[0], x_at[0]
    for back_y in range(4):
        for back_x in range(4):
            first = TEX_ROWS + 8 * back_x
            preds[((y - back_y) & 3) * 4 + ((x - back_x) & 3)] = gots[back_y][first : first + 8].astype(f32)
    table = preds[...].reshape(N_EXP * 8, LANES).astype(bf16)
    place = slot[...]
    lane = place & (LANES - 1)
    pair = place >> 7
    for i in range(CHUNKS):
        row = slice(i, i + 1)
        picked = dot(table, hot(lane[row], LANES))
        owner = jnp.broadcast_to(pair[row] >> 1, (8, LANES))
        total = jnp.where(owner == 0, picked[:8], 0.0)
        for j in range(1, N_EXP):
            total = jnp.where(owner == j, picked[j * 8 : (j + 1) * 8], total)
        predictions[:, i * LANES : (i + 1) * LANES] = jnp.where((pair[row] & 1) == 0, total, pltpu.roll(total, 4, 0))[:OUTC]
    leave(predictions, out_pred)
    for copy in copies:
        copy.wait()


def call(kernel, outs, scratch=(), in_specs=None, flops=0, out_specs=None):
    more = {} if in_specs is None else {"in_specs": in_specs}
    if out_specs is not None:
        more["out_specs"] = out_specs
    cost = pl.CostEstimate(flops=flops, transcendentals=0, bytes_accessed=0) if flops else None
    return pl.pallas_call(
        kernel,
        out_shape=outs,
        scratch_shapes=list(scratch),
        compiler_params=pltpu.CompilerParams(vmem_limit_bytes=32 << 20),
        cost_estimate=cost,
        **more,
    )


def shape(dims, kind=f32):
    return jax.ShapeDtypeStruct(dims, kind)


def on_device(
    latents,
    latent_mean,
    latent_square,
    weight_one,
    weight_two,
    weight_three,
    dir_table,
    materials,
    tile_ids,
    texel_ids,
    dir_ids,
    targets,
):
    flat = lambda a: a.reshape(TEX_ROWS, LANES)
    rows = lambda a: a.reshape(CHUNKS, LANES)
    hbm = pl.BlockSpec(memory_space=pltpu.HBM)
    vmem = pl.BlockSpec(memory_space=pltpu.VMEM)
    smem = pl.BlockSpec(memory_space=pltpu.SMEM)
    index_rows = pltpu.VMEM((CHUNKS, LANES), jnp.int32)
    send, slot = call(
        route_kernel,
        (shape((N_EXP, SEND_ROWS, LANES), bf16), shape((CHUNKS, LANES), jnp.int32)),
        [index_rows] * 4
        + [pltpu.VMEM((OUTC, ROWS), f32), pltpu.VMEM((TEX_ROWS, LANES), f32), pltpu.SemaphoreType.DMA((6,))],
        [hbm] * 6,
    )(*[
        pltpu.with_memory_space_constraint(a, pltpu.HBM)
        for a in (rows(materials), rows(tile_ids), rows(texel_ids), rows(dir_ids), targets, flat(latents))
    ])
    recv = lax.all_to_all(send, "exp", 0, 0, tiled=True)
    three = jnp.pad(weight_three, ((0, 0), (0, 8 - OUTC), (0, 0)))
    weights = (
        weight_one,
        jnp.swapaxes(weight_one, 1, 2) * 0.5,
        weight_two * 0.5,
        jnp.swapaxes(weight_two, 1, 2) * 0.5,
        three,
        jnp.swapaxes(three, 1, 2) * 0.5,
        dir_table.T,
    )
    core = (lax.axis_index("rep") & 1).astype(jnp.int32).reshape(1)
    at_y = (lax.axis_index("exp") >> 2).astype(jnp.int32).reshape(1)
    at_x = (lax.axis_index("exp") & 3).astype(jnp.int32).reshape(1)
    half = lambda keep, kind: call(
        functools.partial(half_kernel, keep),
        (
            shape((N_REP // 2, GRAD_ROWS, LANES), kind),
            shape((2, LAT, SLOTS), bf16),
            shape((2, 8, SLOTS)),
            shape((2, 8, SLOTS)),
        ),
        [pltpu.VMEM((GROUPS * LAT, LOW), bf16)],
        [smem] + [vmem] * 8,
        2000000000,
    )
    grads_a, back_a, preds_a, index_a = half(False, bf16)(core, recv, *weights)
    from_core = lax.ppermute(grads_a, "rep", [(i, i ^ 1) for i in range(N_REP)])
    grads_b, back_b, preds_b, index_b = half(True, f32)(core, recv, *weights)
    chip = (grads_b + from_core.astype(f32)).astype(bf16)
    chips = [list(range(c, N_REP, 2)) for c in range(2)]
    parts = lax.all_to_all(chip, "rep", 0, 0, tiled=True, axis_index_groups=chips)
    along = lambda step_y, step_x: [
        (4 * y + x, 4 * ((y + step_y) % 4) + (x + step_x) % 4) for y in range(4) for x in range(4)
    ]
    rows_x = call(
        texels_kernel,
        tuple([shape((4, BACK_ROWS, LANES), bf16)] * 4),
        [pltpu.VMEM((4, 4, BACK_ROWS, LANES), bf16)],
        [smem] * 2 + [vmem] * 6,
        2000000000,
    )(core, at_x, back_a, back_b, preds_a, preds_b, index_a, index_b)
    got_x = {d: lax.ppermute(rows_x[d], "exp", along(0, d)) for d in (2, 1, 3)}
    rows_y = call(
        relay_kernel,
        tuple([shape((RELAY_ROWS, LANES), bf16)] * 4),
        (),
        [smem] + [vmem] * 4,
    )(at_y, rows_x[0], got_x[2], got_x[1], got_x[3])
    got_y = {d: lax.ppermute(rows_y[d], "exp", along(d, 0)) for d in (2, 1, 3)}
    own = jnp.sum(parts.astype(f32), axis=0).astype(bf16)
    packed = lax.all_gather(own, "rep", axis=0, tiled=False)
    plane = (TEX_ROWS, LANES)
    outs = (weight_one.shape, weight_two.shape, (OUTC, 4, HID), plane, plane, plane, (OUTC, ROWS))
    grad_one, grad_two, grad_three, new_latents, new_mean, new_square, predictions = call(
        finish_kernel,
        tuple(shape(dims) for dims in outs),
        [pltpu.VMEM(dims, f32) for dims in outs]
        + [pltpu.VMEM((N_EXP, 8, LANES), f32), pltpu.SemaphoreType.DMA((10,))],
        [smem] * 2 + [vmem] * 9,
        0,
        tuple([hbm] * 7),
    )(at_y, at_x, packed, rows_y[0], got_y[2], got_y[1], got_y[3], slot, flat(latents), flat(latent_mean), flat(latent_square))
    grad_three = jnp.swapaxes(grad_three, 0, 1)
    whole = lambda a: a.reshape(latents.shape)
    return (
        whole(new_latents),
        whole(new_mean),
        whole(new_square),
        predictions,
        grad_one,
        grad_two,
        grad_three,
    )


def solution(mesh):
    in_specs = (
        P("rep", None, "exp"),
        P("rep", None, "exp"),
        P("rep", None, "exp"),
        P("exp", None, None),
        P("exp", None, None),
        P("exp", None, None),
        P(),
        P(("rep", "exp"), None),
        P(("rep", "exp")),
        P(("rep", "exp")),
        P(("rep", "exp")),
        P(None, ("rep", "exp")),
    )
    out_specs = (
        P("rep", None, "exp"),
        P("rep", None, "exp"),
        P("rep", None, "exp"),
        P(None, ("rep", "exp")),
        P("exp", None, None),
        P("exp", None, None),
        P("exp", None, None),
    )
    return jax.shard_map(on_device, mesh=mesh, in_specs=in_specs, out_specs=out_specs, check_vma=False)
```
